256 devices in a mesh: cand: 4 (over x), seq: 4 (over y), exp: 16 (over z, core).
Axes of the slice: x: 4, y: 4, z: 8, core: 2. Of those that a mesh axis runs over, the one named last changes fastest.
Arguments:
- queries: bfloat16 [16384, 8192], P(('cand', 'seq', 'exp')), parts along dimension 0, may hold values from -18 to 18
- key_heads: bfloat16 [16384, 512], P(('cand', 'seq', 'exp')), parts along dimension 0, may hold values from -6 to 6
- value_heads: bfloat16 [16384, 512], P(('cand', 'seq', 'exp')), parts along dimension 0, may hold values from -24 to 24
- residual: bfloat16 [16384, 4096], P(('cand', 'seq', 'exp')), parts along dimension 0, may hold values from -18 to 18
- out_weight: bfloat16 [8192, 4096], P(('seq', 'exp')), may hold values from -0.25 to 0.25
- norm_gain: bfloat16 [4096], replicated, may hold values from 0.099609375 to 1.8984375
- gate_weight: bfloat16 [16, 4096, 1536], P('exp', None, 'seq'), may hold values from -0.09375 to 0.09375
- up_weight: bfloat16 [16, 4096, 1536], P('exp', None, 'seq'), may hold values from -0.09375 to 0.09375
- down_weight: bfloat16 [16, 1536, 4096], P('exp', 'seq'), may hold values from -0.15625 to 0.15625
- expert_ids: int32 [16384, 2], P(('cand', 'seq', 'exp')), parts along dimension 0, may hold values from 0 to 15, all different within a row; in each aligned block of 64 rows (0 to 63, 64 to 127, ...) at most 12 rows name the same one
- route_gates: float32 [16384, 2], P(('cand', 'seq', 'exp')), parts along dimension 0, may hold values from 0.1 to 1
Outputs:
- layer_out: bfloat16 [16384, 4096], P(('cand', 'seq', 'exp')), parts along dimension 0
The draws below stay inside these ranges and needn't reach their ends.
There are 4 independent parts, one for each index of `cand`. The reference program is written for one: setup_inputs(seed, part) draws one part's arguments, and reference() takes and returns one part's arrays. A program takes and returns all parts, laid end to end along the dimension named above; an argument that names none is the same for every part. Nothing has to cross between parts.
Inputs may be any that keep to these rules, and one draw needn't show every extreme that they name: `expert_ids`: A row names 2 different experts. In each aligned block of 64 rows (the rows of one device) no expert is named by more than 12 rows, a bound that some block reaches.
All inputs are finite; a program needn't handle non-finite values.
Results may differ from the reference program's by a relative error of at most 0.022.
Values may be sent and summed in bfloat16 or wider, within the bound.
No kernel may reach another device: no remote copies, remote signals or barrier semaphores. Data moves between devices by JAX's collectives and lax.ppermute only.
A program may use at most 128 MiB of HBM per device.

```python
import math
import jax
import jax.numpy as jnp
import numpy as np
from jax import lax

D = 4096
HEADS = 64
KV_HEADS = 4
HEAD_DIM = 128
FF = 1536
TOP = 2
TOK_DEV = 64
SEQ = 4096
EXPERTS = 16
HEADS_DEV = 1
CAP = 12
N_SEQ = 4
N_EXP = 16


def query_key_pair(key):
    query_key = jax.random.fold_in(key, 11)
    key_key = jax.random.fold_in(key, 12)
    keys_out = jnp.clip(jax.random.normal(key_key, (SEQ, KV_HEADS, HEAD_DIM), jnp.float32), -5.0, 5.0)
    queries_out = jnp.clip(jax.random.normal(query_key, (SEQ, HEADS, HEAD_DIM), jnp.float32), -5.0, 5.0)
    return (queries_out.reshape(SEQ, HEADS * HEAD_DIM), keys_out.reshape(SEQ, KV_HEADS * HEAD_DIM))


def draw_queries(key, part):
    return query_key_pair(key)[0].astype(jnp.bfloat16)


def draw_key_heads(key, part):
    return query_key_pair(key)[1].astype(jnp.bfloat16)


def draw_residual(key, part):
    base_key = jax.random.fold_in(key, 21)
    row_key = jax.random.fold_in(key, 22)
    col_key = jax.random.fold_in(key, 23)
    row_scale = jnp.exp(jax.random.uniform(row_key, (SEQ, 1), jnp.float32, math.log(0.3), math.log(3.0)))
    col_scale = jnp.exp(jax.random.uniform(col_key, (1, D), jnp.float32, math.log(0.5), math.log(2.0)))
    base = jnp.clip(jax.random.normal(base_key, (SEQ, D), jnp.float32), -3.0, 3.0)
    return (base * row_scale * col_scale).astype(jnp.bfloat16)


def block_scale(own_key, dims, split, least, top_value):
    factor_of = 1.0
    for dim, shards_of in split:
        steps = jax.random.uniform(jax.random.fold_in(jax.random.fold_in(own_key, 6), dim), (shards_of,), jnp.float32, least / len(split), top_value / len(split))
        factor_of = factor_of * jnp.repeat(jnp.exp(steps), dims[dim] // shards_of).reshape((-1,) + (1,) * (len(dims) - 1 - dim))
    return factor_of


def shared_out(own_key, own, number, rows, number_of, top, most, lean):
    order = jax.random.permutation(own_key, number_of)
    crowded, common = load_shares(number_of, rows * top, most, lean, True), load_shares(number_of, rows * top, most, lean, False)
    places = jnp.arange(number_of)

    def named(lengths, turn):
        used = int((lengths > 0).sum())
        fixed = max(1, used // 4)
        moved = fixed + (places - fixed + turn * (used - fixed)) % max(1, number_of - fixed)
        return jnp.zeros((number_of,), jnp.int32).at[order[jnp.where(places < fixed, places, moved)]].set(jnp.asarray(lengths, jnp.int32))

    lengths = jnp.where(number % 4 == 0, named(crowded, number // 4), named(common, number - number // 4 - 1))
    mixed = jax.random.permutation(jax.random.fold_in(own, 3), number_of)
    source_of, receiver = mixed[0:number_of // 2 * 2:2], mixed[1:number_of // 2 * 2:2]
    slack = jnp.minimum(lengths[source_of] - 1, most - lengths[receiver]) // 2
    slack = jnp.where((source_of == order[0]) | (receiver == order[0]) | (lengths[receiver] == 0), 0, jnp.maximum(slack, 0))
    moved = jax.random.randint(jax.random.fold_in(own, 4), (number_of // 2,), 0, 1 << 20) % (slack + 1)
    lengths = lengths.at[source_of].add(-moved).at[receiver].add(moved)
    labels = jnp.searchsorted(jnp.cumsum(lengths), jnp.arange(rows * top), side="right").astype(jnp.int32)
    grid = labels.reshape(top, rows).T
    grid = grid[jax.random.permutation(jax.random.fold_in(own, 1), rows)]
    turn = jax.random.randint(jax.random.fold_in(own, 2), (rows, 1), 0, top)
    return jnp.take_along_axis(grid, (jnp.arange(top)[None, :] + turn) % top, axis=1)


def load_shares(amount, total, limit, skew, full):
    weights = [(1 << 20) // math.isqrt(rank ** skew) + 1 for rank in range(1, amount + 1)]
    largest = limit if full else min(limit, max(-(-total // amount), total * weights[0] // sum(weights)))
    least = 1 if total - largest >= amount - 1 else 0
    given, rest = [largest] + [least] * (amount - 1), total - largest - least * (amount - 1)
    while rest > 0:
        free = [i for i in range(1, amount) if given[i] < largest] or [i for i in range(1, amount) if given[i] < limit]
        mass, left = sum([weights[i] for i in free]), rest
        for i in free:
            extra = min(limit - given[i], max(1, left * weights[i] // mass), rest)
            given[i] = given[i] + extra
            rest = rest - extra
    return np.array(given)


def normal_values(key, dims, deviation, limit, cuts=(), kind=jnp.bfloat16):
    drawn = jax.random.normal(key, dims, jnp.float32) * deviation
    if len(cuts) > 0:
        drawn = block_scale(key, dims, cuts, -0.22, 0.18) * drawn
    return jnp.clip(drawn, min=-limit, max=limit).astype(kind)


def setup_inputs(seed: int = 0, part: int = 0) -> dict:
    key_of = jax.random.split(jax.random.key(seed), 12)
    part_keys = jax.random.split(jax.random.fold_in(key_of[11], part), 12)
    queries = draw_queries(jax.random.fold_in(jax.random.fold_in(key_of[11], part), 71), part)
    key_heads = draw_key_heads(jax.random.fold_in(jax.random.fold_in(key_of[11], part), 71), part)
    value_heads = normal_values(part_keys[2], (SEQ, KV_HEADS * HEAD_DIM), 4.0, 24.0, ((0, 64),))
    residual = draw_residual(jax.random.fold_in(jax.random.fold_in(key_of[11], part), 71), part)
    out_weight = normal_values(key_of[4], (HEADS * HEAD_DIM, D), (KV_HEADS * HEAD_DIM) ** -0.5, 0.25, ((0, 64),))
    norm_gain = jnp.clip(1.0 + 0.18 * jax.random.normal(key_of[5], (D,), jnp.float32), 0.099609375, 1.8984375).astype(jnp.bfloat16)
    gate_weight = normal_values(key_of[6], (EXPERTS, D, FF), D ** -0.5, 0.09375, ((0, 16), (2, 4)))
    up_weight = normal_values(key_of[7], (EXPERTS, D, FF), D ** -0.5, 0.09375, ((0, 16), (2, 4)))
    down_weight = normal_values(key_of[8], (EXPERTS, FF, D), FF ** -0.5, 0.15625, ((0, 16), (1, 4)))
    expert_ids_keys = jax.random.split(jax.random.fold_in(part_keys[9], 1), SEQ // TOK_DEV)
    expert_ids_turns = jax.random.permutation(jax.random.fold_in(part_keys[9], 3), SEQ // TOK_DEV)
    expert_ids = jax.vmap(lambda own, number: shared_out(jax.random.fold_in(part_keys[9], 2), own, number, TOK_DEV, EXPERTS, TOP, CAP, 2))(expert_ids_keys, expert_ids_turns).reshape((SEQ, TOP))
    route_gates = jnp.clip(jnp.exp(math.log(1.0) - 2.3025851 * jax.random.uniform(part_keys[10], (SEQ, TOP), jnp.float32) ** block_scale(part_keys[10], (SEQ, TOP), ((0, 64),), -0.2, 0.2)), 0.1, 1.0)
    return {"queries": queries, "key_heads": key_heads, "value_heads": value_heads, "residual": residual, "out_weight": out_weight, "norm_gain": norm_gain, "gate_weight": gate_weight, "up_weight": up_weight, "down_weight": down_weight, "expert_ids": expert_ids, "route_gates": route_gates}


norm_eps = 1e-06

def attend_head(query_head, key_head, value_head):
    span_rows = min(512, SEQ)
    inv_scale = 1.0 / HEAD_DIM ** 0.5
    results = []
    for offset in range(0, SEQ, span_rows):
        query_part = query_head[offset:offset + span_rows]
        key_part = key_head[:offset + span_rows]
        value_part = value_head[:offset + span_rows]
        scores = jnp.dot(query_part, key_part.T, preferred_element_type=jnp.float32) * inv_scale
        row_pos = offset + jnp.arange(span_rows, dtype=jnp.int32)[:, None]
        col_pos = jnp.arange(offset + span_rows, dtype=jnp.int32)[None, :]
        scores = jnp.where(col_pos <= row_pos, scores, -jnp.inf)
        row_max = lax.optimization_barrier(jnp.max(scores, axis=1, keepdims=True))
        weights = jnp.exp(scores - row_max)
        shares = (weights / lax.optimization_barrier(jnp.sum(weights, axis=1, keepdims=True))).astype(jnp.bfloat16)
        results.append(jnp.dot(shares, value_part, preferred_element_type=jnp.float32).astype(jnp.bfloat16))
    return jnp.concatenate(results, axis=0)

def reference(queries, key_heads, value_heads, residual, out_weight, norm_gain, gate_weight, up_weight, down_weight, expert_ids, route_gates):
    group_size = HEADS // KV_HEADS
    query_stack = queries.reshape(SEQ, HEADS, HEAD_DIM).transpose(1, 0, 2)
    key_stack = key_heads.reshape(SEQ, KV_HEADS, HEAD_DIM).transpose(1, 0, 2)
    value_stack = value_heads.reshape(SEQ, KV_HEADS, HEAD_DIM).transpose(1, 0, 2)

    def one_head(head):
        return attend_head(query_stack[head], key_stack[head // group_size], value_stack[head // group_size])
    attended = lax.map(one_head, jnp.arange(HEADS, dtype=jnp.int32))
    attended = attended.transpose(1, 0, 2).reshape(SEQ, N_SEQ, N_EXP, HEADS_DEV * HEAD_DIM)
    weight_groups = out_weight.reshape(N_SEQ, N_EXP, HEADS_DEV * HEAD_DIM, D)

    def add_group(index, total):
        head_cols = attended[:, :, index, :].reshape(SEQ, N_SEQ * HEADS_DEV * HEAD_DIM)
        weight_rows = weight_groups[:, index].reshape(N_SEQ * HEADS_DEV * HEAD_DIM, D)
        group_part = jnp.dot(head_cols, weight_rows, preferred_element_type=jnp.float32).astype(jnp.bfloat16)
        group_part = lax.optimization_barrier(group_part)
        return total + group_part.astype(jnp.float32)
    projected = lax.fori_loop(0, N_EXP, add_group, jnp.zeros((SEQ, D), jnp.float32))
    hidden = residual.astype(jnp.float32) + projected
    mean_square = lax.optimization_barrier(jnp.mean(hidden * hidden, axis=1, keepdims=True))
    normed = (hidden * lax.rsqrt(mean_square + norm_eps) * norm_gain.astype(jnp.float32)).astype(jnp.bfloat16)
    blocks = SEQ // TOK_DEV
    flat_ids = expert_ids.reshape(blocks, TOK_DEV * TOP)
    matches = (flat_ids[:, :, None] == jnp.arange(EXPERTS, dtype=jnp.int32)[None, None, :]).astype(jnp.int32)
    before = jnp.cumsum(matches, axis=1) - matches
    slot_rank = lax.optimization_barrier(jnp.sum(before * matches, axis=2)).astype(jnp.int32)
    block_index = jnp.arange(blocks, dtype=jnp.int32)[:, None]
    token_index = jnp.arange(TOK_DEV * TOP, dtype=jnp.int32) // TOP
    sources = normed.reshape(blocks, TOK_DEV, D)[:, token_index]
    buffer = jnp.zeros((EXPERTS, blocks, CAP, D), jnp.bfloat16)
    buffer = buffer.at[flat_ids, block_index, slot_rank].set(sources)
    quarter_width = FF // N_SEQ

    def run_expert(expert):
        token_rows = buffer[expert].reshape(blocks * CAP, D)
        gate_act = jnp.dot(token_rows, gate_weight[expert], preferred_element_type=jnp.float32)
        up_act = jnp.dot(token_rows, up_weight[expert], preferred_element_type=jnp.float32)
        hidden_act = (jax.nn.silu(gate_act) * up_act).astype(jnp.bfloat16)
        total = jnp.zeros((blocks * CAP, D), jnp.float32)
        for quarter in range(N_SEQ):
            low = quarter * quarter_width
            expert_part = jnp.dot(hidden_act[:, low:low + quarter_width], down_weight[expert, low:low + quarter_width], preferred_element_type=jnp.float32).astype(jnp.bfloat16)
            expert_part = lax.optimization_barrier(expert_part)
            total = total + expert_part.astype(jnp.float32)
        return total.astype(jnp.bfloat16)
    expert_out = lax.map(run_expert, jnp.arange(EXPERTS, dtype=jnp.int32)).reshape(EXPERTS, blocks, CAP, D)
    picked = expert_out[flat_ids, block_index, slot_rank].reshape(SEQ, TOP, D)
    blended = lax.optimization_barrier(jnp.sum(picked.astype(jnp.float32) * route_gates[:, :, None], axis=1))
    return (hidden + blended).astype(jnp.bfloat16)
```

```python
import jax
import jax.numpy as jnp
from jax import lax
from jax.sharding import PartitionSpec as P

HEAD_DIM = 128


norm_eps = 1e-06


def attend(query_rows, key_rows, value_rows):
    seq_len, head_width = query_rows.shape
    head_count = head_width // HEAD_DIM
    span_rows = min(512, seq_len)
    inv_scale = 1.0 / HEAD_DIM**0.5
    results = []
    for offset in range(0, seq_len, span_rows):
        query_part = query_rows[offset : offset + span_rows].reshape(
            span_rows, head_count, HEAD_DIM
        )
        key_part = key_rows[: offset + span_rows]
        value_part = value_rows[: offset + span_rows]
        scores = (
            jnp.einsum("qhd,kd->hqk", query_part, key_part, preferred_element_type=jnp.float32)
            * inv_scale
        )
        row_pos = offset + lax.broadcasted_iota(jnp.int32, (span_rows, offset + span_rows), 0)
        col_pos = lax.broadcasted_iota(jnp.int32, (span_rows, offset + span_rows), 1)
        scores = jnp.where((col_pos <= row_pos)[None], scores, -jnp.inf)
        row_max = jnp.max(scores, axis=2, keepdims=True)
        weights = jnp.exp(scores - row_max)
        shares = (weights / jnp.sum(weights, axis=2, keepdims=True)).astype(jnp.bfloat16)
        blended = jnp.einsum("hqk,kd->qhd", shares, value_part, preferred_element_type=jnp.float32)
        results.append(blended.astype(jnp.bfloat16).reshape(span_rows, head_width))
    return jnp.concatenate(results, axis=0)


def slot_targets(expert_ids, experts, capacity):
    tokens, fanout = expert_ids.shape
    entries = tokens * fanout
    flat_ids = expert_ids.reshape(entries)
    same_expert = flat_ids[:, None] == flat_ids[None, :]
    earlier = lax.broadcasted_iota(jnp.int32, (entries, entries), 1) < lax.broadcasted_iota(
        jnp.int32, (entries, entries), 0
    )
    slot_rank = jnp.sum((same_expert & earlier).astype(jnp.int32), axis=1)
    return flat_ids * capacity + slot_rank


def expert_term(token_rows, gate_weight, up_weight, down_weight):
    gate_act = jnp.dot(token_rows, gate_weight[0], preferred_element_type=jnp.float32)
    up_act = jnp.dot(token_rows, up_weight[0], preferred_element_type=jnp.float32)
    hidden_act = (jax.nn.silu(gate_act) * up_act).astype(jnp.bfloat16)
    return jnp.dot(hidden_act, down_weight[0], preferred_element_type=jnp.float32)


def body(
    queries,
    key_heads,
    value_heads,
    residual,
    out_weight,
    norm_gain,
    gate_weight,
    up_weight,
    down_weight,
    expert_ids,
    route_gates,
):
    tokens, model_width = residual.shape
    seq_size = lax.axis_size("seq")
    exp_size = lax.axis_size("exp")
    query_rows = lax.all_to_all(queries, ("seq", "exp"), split_axis=1, concat_axis=0, tiled=True)
    key_local, value_local = (
        lax.all_gather(key_heads, "exp", axis=0, tiled=True),
        lax.all_gather(value_heads, "exp", axis=0, tiled=True),
    )
    key_rows, value_rows = (
        lax.all_to_all(key_local, "seq", split_axis=1, concat_axis=0, tiled=True),
        lax.all_to_all(value_local, "seq", split_axis=1, concat_axis=0, tiled=True),
    )
    attended = attend(query_rows, key_rows, value_rows)
    head_cols = lax.all_to_all(attended, "seq", split_axis=0, concat_axis=1, tiled=True)
    weight_rows = lax.all_gather(out_weight, "seq", axis=0, tiled=True)
    projected = lax.psum_scatter(
        jnp.dot(head_cols, weight_rows, preferred_element_type=jnp.float32).astype(jnp.bfloat16),
        "exp",
        scatter_dimension=0,
        tiled=True,
    ).astype(jnp.float32)
    hidden = residual.astype(jnp.float32) + projected
    mean_square = jnp.mean(hidden * hidden, axis=1, keepdims=True)
    normed = (hidden * lax.rsqrt(mean_square + norm_eps) * norm_gain.astype(jnp.float32)).astype(
        jnp.bfloat16
    )
    fanout = expert_ids.shape[1]
    capacity = min(tokens, 3 * tokens * fanout // (2 * exp_size))
    targets = slot_targets(expert_ids, exp_size, capacity)
    slot_count = exp_size * capacity
    dispatch_map = jnp.sum(
        (
            lax.broadcasted_iota(jnp.int32, (slot_count, tokens, fanout), 0)
            == targets.reshape(1, tokens, fanout)
        ).astype(jnp.int32),
        axis=2,
    )
    outgoing = jnp.dot(
        dispatch_map.astype(jnp.bfloat16), normed, preferred_element_type=jnp.float32
    ).astype(jnp.bfloat16)
    outgoing = outgoing.reshape(exp_size, capacity, model_width)
    arrived = lax.all_to_all(outgoing, "exp", split_axis=0, concat_axis=0, tiled=True)
    everyone = lax.all_gather(arrived, "seq", axis=0, tiled=True).reshape(
        seq_size * slot_count, model_width
    )
    summed = lax.psum_scatter(
        expert_term(everyone, gate_weight, up_weight, down_weight).astype(jnp.bfloat16),
        "seq",
        scatter_dimension=0,
        tiled=True,
    )
    returned = lax.all_to_all(
        summed.reshape(exp_size, capacity, model_width),
        "exp",
        split_axis=0,
        concat_axis=0,
        tiled=True,
    )
    expert_out = returned.reshape(slot_count, model_width)
    picked = jnp.take(expert_out, targets, axis=0).reshape(tokens, fanout, model_width)
    blended = jnp.sum(picked.astype(jnp.float32) * route_gates[:, :, None], axis=1)
    return (hidden + blended).astype(jnp.bfloat16)


def solution(mesh):
    placed = (
        P(("cand", "seq", "exp"), None),
        P(("cand", "seq", "exp"), None),
        P(("cand", "seq", "exp"), None),
        P(("cand", "seq", "exp"), None),
        P(("seq", "exp"), None),
        P(),
        P("exp", None, "seq"),
        P("exp", None, "seq"),
        P("exp", "seq", None),
        P(("cand", "seq", "exp"), None),
        P(("cand", "seq", "exp"), None),
    )
    return jax.shard_map(
        body, mesh=mesh, in_specs=placed, out_specs=P(("cand", "seq", "exp"), None), check_vma=False
    )
```

```python
import math

import jax
import jax.numpy as jnp
from jax import lax
from jax.experimental import pallas as pl
from jax.experimental.pallas import tpu as pltpu
from jax.sharding import PartitionSpec as P

HEAD_DIM = 128
BLOCK = 512
HALVES = 2

norm_eps = 1e-06


def attention_kernel(query_ref, pair_ref, out_ref):
    block = pl.program_id(0)
    rows = query_ref.shape[0]
    part = rows // 2
    factor = math.log2(math.e) / HEAD_DIM**0.5
    parts = [query_ref[index * part : (index + 1) * part, :] for index in range(2)]

    def scores_of(start, queries):
        keys = pair_ref[pl.ds(start, rows), :HEAD_DIM]
        return lax.dot_general(
            keys, queries, (((1,), (1,)), ((), ())), preferred_element_type=jnp.float32
        )

    def mix(start, shares):
        values = pair_ref[pl.ds(start, rows), HEAD_DIM:]
        return lax.dot_general(
            values, shares, (((0,), (0,)), ((), ())), preferred_element_type=jnp.float32
        )

    first = pl.multiple_of(block * rows, rows)
    carry = []
    for index in range(2):
        scores = scores_of(first, parts[index])
        key_pos = lax.broadcasted_iota(jnp.int32, (rows, part), 0)
        query_pos = index * part + lax.broadcasted_iota(jnp.int32, (rows, part), 1)
        scores = jnp.where(key_pos <= query_pos, scores, -1e30)
        top = jnp.max(scores, axis=0, keepdims=True)
        weights = jnp.exp2(scores * factor - top * factor)
        total = jnp.sum(weights, axis=0, keepdims=True)
        carry += [top, total, mix(first, weights.astype(jnp.bfloat16))]

    def step(turn, carry):
        start = pl.multiple_of(turn * rows, rows)
        after = []
        scores_both = [scores_of(start, parts[index]) for index in range(2)]
        for index in range(2):
            top, total, mixed = carry[3 * index : 3 * index + 3]
            scores = scores_both[index]
            new_top = jnp.maximum(top, jnp.max(scores, axis=0, keepdims=True))
            weights = jnp.exp2(scores * factor - new_top * factor)
            shrink = jnp.exp2((top - new_top) * factor)
            after += [
                new_top,
                total * shrink + jnp.sum(weights, axis=0, keepdims=True),
                mixed * shrink + mix(start, weights.astype(jnp.bfloat16)),
            ]
        return tuple(after)

    carry = lax.fori_loop(0, block, step, tuple(carry))
    for index in range(2):
        top, total, mixed = carry[3 * index : 3 * index + 3]
        out_ref[index * part : (index + 1) * part, :] = (
            (mixed * (1.0 / total)).T.astype(jnp.bfloat16)
        )


def attend(query_rows, pair_rows):
    seq_len = query_rows.shape[0]
    return pl.pallas_call(
        attention_kernel,
        grid=(seq_len // BLOCK,),
        in_specs=[
            pl.BlockSpec((BLOCK, HEAD_DIM), lambda index: (index, 0)),
            pl.BlockSpec((seq_len, 2 * HEAD_DIM), lambda index: (0, 0)),
        ],
        out_specs=pl.BlockSpec((BLOCK, HEAD_DIM), lambda index: (index, 0)),
        out_shape=jax.ShapeDtypeStruct((seq_len, HEAD_DIM), jnp.bfloat16),
        compiler_params=pltpu.CompilerParams(vmem_limit_bytes=40 * 1024 * 1024),
        name="attention",
    )(query_rows, pair_rows)


def slot_targets(expert_ids, capacity):
    tokens, fanout = expert_ids.shape
    entries = tokens * fanout
    flat_ids = expert_ids.reshape(entries)
    same_expert = flat_ids[:, None] == flat_ids[None, :]
    earlier = lax.broadcasted_iota(jnp.int32, (entries, entries), 1) < lax.broadcasted_iota(
        jnp.int32, (entries, entries), 0
    )
    slot_rank = jnp.sum((same_expert & earlier).astype(jnp.int32), axis=1)
    return (flat_ids * capacity + slot_rank).reshape(tokens, fanout)


def sent_rows(shape, dim, capacity):
    row = lax.broadcasted_iota(jnp.int32, shape, dim)
    within = row % (HALVES * capacity)
    return row // (HALVES * capacity) * capacity + within % capacity, within // capacity


def body(
    queries,
    key_heads,
    value_heads,
    residual,
    out_weight,
    norm_gain,
    gate_weight,
    up_weight,
    down_weight,
    expert_ids,
    route_gates,
):
    tokens, model_width = residual.shape
    seq_size = lax.axis_size("seq")
    exp_size = lax.axis_size("exp")
    half_width = model_width // HALVES
    fanout = expert_ids.shape[1]
    capacity = min(tokens, 3 * tokens * fanout // (2 * exp_size))
    slot_count = exp_size * capacity
    sent_count = HALVES * slot_count

    pairs = jnp.concatenate(
        [
            key_heads.reshape(tokens, seq_size, HEAD_DIM),
            value_heads.reshape(tokens, seq_size, HEAD_DIM),
        ],
        axis=2,
    ).reshape(tokens, seq_size * 2 * HEAD_DIM)
    pair_local = lax.all_to_all(pairs, "seq", split_axis=1, concat_axis=0, tiled=True)
    pair_local = pair_local.reshape(seq_size, tokens, 2 * HEAD_DIM)
    query_rows = lax.all_to_all(queries, ("seq", "exp"), split_axis=1, concat_axis=0, tiled=True)
    pair_rows = lax.all_gather(pair_local, "exp", axis=1, tiled=True).reshape(
        seq_size * exp_size * tokens, 2 * HEAD_DIM
    )
    weight_rows = lax.all_gather(out_weight, "seq", axis=0, tiled=True)
    attended = attend(query_rows, pair_rows)
    head_cols = lax.all_to_all(attended, "seq", split_axis=0, concat_axis=1, tiled=True)
    projected = lax.psum_scatter(
        jnp.dot(head_cols, weight_rows, preferred_element_type=jnp.float32).astype(jnp.bfloat16),
        "exp",
        scatter_dimension=0,
        tiled=True,
    ).astype(jnp.float32)
    hidden = residual.astype(jnp.float32) + projected
    mean_square = jnp.mean(hidden * hidden, axis=1, keepdims=True)
    normed = (hidden * lax.rsqrt(mean_square + norm_eps) * norm_gain.astype(jnp.float32)).astype(
        jnp.bfloat16
    )

    targets = slot_targets(expert_ids, capacity)
    token_pairs = jnp.tile(targets, (HALVES, 1))
    gate_pairs = jnp.tile(route_gates, (HALVES, 1))
    pair_half = lax.broadcasted_iota(jnp.int32, (sent_count, HALVES * tokens), 1) // tokens
    slot_of, half_of = sent_rows((sent_count, HALVES * tokens), 0, capacity)
    here = [(token_pairs[:, k][None, :] == slot_of) & (half_of == pair_half) for k in range(fanout)]
    send_map = sum(hit.astype(jnp.float32) for hit in here).astype(jnp.bfloat16)
    blend_map = sum(
        jnp.where(hit, gate_pairs[:, k][None, :], 0.0) for k, hit in enumerate(here)
    )
    blend_high = blend_map.astype(jnp.bfloat16)
    blend_low = (blend_map - blend_high.astype(jnp.float32)).astype(jnp.bfloat16)
    row_slot, row_half = sent_rows((sent_count, sent_count), 1, capacity)
    plain_row = lax.broadcasted_iota(jnp.int32, (sent_count, sent_count), 0)
    order_map = (plain_row == row_half * slot_count + row_slot).astype(jnp.bfloat16)

    stacked = jnp.concatenate([normed[:, :half_width], normed[:, half_width:]], axis=0)
    outgoing = jnp.dot(send_map, stacked, preferred_element_type=jnp.float32).astype(jnp.bfloat16)
    arrived = lax.all_to_all(outgoing, "exp", split_axis=0, concat_axis=0, tiled=True)
    everyone = lax.all_gather(arrived, "seq", axis=0, tiled=True)
    everyone = everyone.reshape(seq_size, sent_count, half_width)
    ordered = [
        jnp.einsum(
            "rk,bkd->brd",
            order_map[half * slot_count : (half + 1) * slot_count],
            everyone,
            preferred_element_type=jnp.float32,
        )
        .astype(jnp.bfloat16)
        .reshape(seq_size * slot_count, half_width)
        for half in range(HALVES)
    ]

    def widen(weight):
        return jnp.dot(
            ordered[0], weight[0, :half_width], preferred_element_type=jnp.float32
        ) + jnp.dot(ordered[1], weight[0, half_width:], preferred_element_type=jnp.float32)

    hidden_act = (jax.nn.silu(widen(gate_weight)) * widen(up_weight)).astype(jnp.bfloat16)
    expert_part = jnp.dot(hidden_act, down_weight[0], preferred_element_type=jnp.float32).astype(
        jnp.bfloat16
    )
    summed = lax.psum_scatter(
        expert_part,
        "seq",
        scatter_dimension=0,
        tiled=True,
    )
    stacked_out = jnp.concatenate([summed[:, :half_width], summed[:, half_width:]], axis=0)
    leaving = lax.dot_general(
        order_map, stacked_out, (((0,), (0,)), ((), ())), preferred_element_type=jnp.float32
    ).astype(jnp.bfloat16)
    returned = lax.all_to_all(leaving, "exp", split_axis=0, concat_axis=0, tiled=True)
    blended = sum(
        lax.dot_general(part, returned, (((0,), (0,)), ((), ())), preferred_element_type=jnp.float32)
        for part in (blend_high, blend_low)
    )
    blended = jnp.concatenate([blended[:tokens], blended[tokens:]], axis=1)
    return (hidden + blended).astype(jnp.bfloat16)


def solution(mesh):
    placed = (
        P(("cand", "seq", "exp"), None),
        P(("cand", "seq", "exp"), None),
        P(("cand", "seq", "exp"), None),
        P(("cand", "seq", "exp"), None),
        P(("seq", "exp"), None),
        P(),
        P("exp", None, "seq"),
        P("exp", None, "seq"),
        P("exp", "seq", None),
        P(("cand", "seq", "exp"), None),
        P(("cand", "seq", "exp"), None),
    )
    return jax.shard_map(
        body, mesh=mesh, in_specs=placed, out_specs=P(("cand", "seq", "exp"), None), check_vma=False
    )
```

```python
import math

import jax
import jax.numpy as jnp
from jax import lax
from jax.experimental import pallas as pl
from jax.experimental.pallas import tpu as pltpu
from jax.sharding import PartitionSpec as P

HEAD_DIM = 128
BLOCK = 512
PARTS = 4

norm_eps = 1e-06


def attention_kernel(query_ref, pair_ref, out_ref):
    block = pl.program_id(0)
    rows = query_ref.shape[0]
    part = rows // 2
    factor = math.log2(math.e) / HEAD_DIM**0.5
    parts = [query_ref[index * part : (index + 1) * part, :] for index in range(2)]

    def scores_of(start, queries):
        keys = pair_ref[pl.ds(start, rows), :HEAD_DIM]
        return lax.dot_general(
            keys, queries, (((1,), (1,)), ((), ())), preferred_element_type=jnp.float32
        )

    def mix(start, shares):
        values = pair_ref[pl.ds(start, rows), HEAD_DIM:]
        return lax.dot_general(
            values, shares, (((0,), (0,)), ((), ())), preferred_element_type=jnp.float32
        )

    first = pl.multiple_of(block * rows, rows)
    carry = []
    for index in range(2):
        scores = scores_of(first, parts[index])
        key_pos = lax.broadcasted_iota(jnp.int32, (rows, part), 0)
        query_pos = index * part + lax.broadcasted_iota(jnp.int32, (rows, part), 1)
        scores = jnp.where(key_pos <= query_pos, scores, -1e30)
        top = jnp.max(scores, axis=0, keepdims=True)
        weights = jnp.exp2(scores * factor - top * factor)
        total = jnp.sum(weights, axis=0, keepdims=True)
        carry += [top, total, mix(first, weights.astype(jnp.bfloat16))]

    def step(turn, carry):
        start = pl.multiple_of(turn * rows, rows)
        after = []
        scores_both = [scores_of(start, parts[index]) for index in range(2)]
        for index in range(2):
            top, total, mixed = carry[3 * index : 3 * index + 3]
            scores = scores_both[index]
            new_top = jnp.maximum(top, jnp.max(scores, axis=0, keepdims=True))
            weights = jnp.exp2(scores * factor - new_top * factor)
            shrink = jnp.exp2((top - new_top) * factor)
            after += [
                new_top,
                total * shrink + jnp.sum(weights, axis=0, keepdims=True),
                mixed * shrink + mix(start, weights.astype(jnp.bfloat16)),
            ]
        return tuple(after)

    carry = lax.fori_loop(0, block, step, tuple(carry))
    for index in range(2):
        top, total, mixed = carry[3 * index : 3 * index + 3]
        out_ref[index * part : (index + 1) * part, :] = (
            (mixed * (1.0 / total)).T.astype(jnp.bfloat16)
        )


def attend(query_rows, pair_rows):
    seq_len = query_rows.shape[0]
    return pl.pallas_call(
        attention_kernel,
        grid=(seq_len // BLOCK,),
        in_specs=[
            pl.BlockSpec((BLOCK, HEAD_DIM), lambda index: (index, 0)),
            pl.BlockSpec((seq_len, 2 * HEAD_DIM), lambda index: (0, 0)),
        ],
        out_specs=pl.BlockSpec((BLOCK, HEAD_DIM), lambda index: (index, 0)),
        out_shape=jax.ShapeDtypeStruct((seq_len, HEAD_DIM), jnp.bfloat16),
        compiler_params=pltpu.CompilerParams(vmem_limit_bytes=40 * 1024 * 1024),
        name="attention",
    )(query_rows, pair_rows)


def slot_targets(expert_ids, capacity):
    tokens, fanout = expert_ids.shape
    entries = tokens * fanout
    flat_ids = expert_ids.reshape(entries)
    same_expert = flat_ids[:, None] == flat_ids[None, :]
    earlier = lax.broadcasted_iota(jnp.int32, (entries, entries), 1) < lax.broadcasted_iota(
        jnp.int32, (entries, entries), 0
    )
    slot_rank = jnp.sum((same_expert & earlier).astype(jnp.int32), axis=1)
    return (flat_ids * capacity + slot_rank).reshape(tokens, fanout)


def sent_rows(shape, dim, capacity):
    row = lax.broadcasted_iota(jnp.int32, shape, dim)
    within = row % (PARTS * capacity)
    return row // (PARTS * capacity) * capacity + within % capacity, within // capacity


def shift(array, axis, distance):
    size = lax.axis_size(axis)
    return lax.ppermute(array, axis, [(i, (i + distance) % size) for i in range(size)])


def pass_kernel(*refs):
    del refs


def meet(*arrays):
    anywhere = pl.BlockSpec(memory_space=pl.ANY)
    return pl.pallas_call(
        pass_kernel,
        in_specs=[anywhere] * len(arrays),
        out_specs=[anywhere] * len(arrays),
        out_shape=[jax.ShapeDtypeStruct(array.shape, array.dtype) for array in arrays],
        input_output_aliases={index: index for index in range(len(arrays))},
        name="meet",
    )(*arrays)


def expert_kernel(order_ref, rows_ref, *refs):
    gate_own, up_own = refs[:2]
    gate_up = refs[2:13]
    down_parts = refs[15:20]
    out_ref, gate_buf, up_buf, down_buf, sems = refs[20:]
    depth = rows_ref.shape[2]
    half = down_buf.shape[2] // 2
    moves = []

    def fetch(source, target):
        move = pltpu.make_async_copy(source, target, sems.at[len(moves)])
        move.start()
        moves.append(move)

    for part in range(PARTS):
        start = pl.multiple_of(order_ref[part] * depth, depth)
        fetch(gate_own.at[pl.ds(start, depth)], gate_buf.at[0, part])
        fetch(up_own.at[pl.ds(start, depth)], up_buf.at[0, part])
    for index, piece in enumerate(gate_up):
        quarter, part = 1 + index // PARTS, index % PARTS
        fetch(piece.at[pl.ds(0, depth)], gate_buf.at[quarter, part])
        fetch(piece.at[pl.ds(depth, depth)], up_buf.at[quarter, part])
    fetch(refs[13], gate_buf.at[3, PARTS - 1])
    fetch(refs[14], up_buf.at[3, PARTS - 1])
    for quarter in range(3):
        fetch(down_parts[quarter], down_buf.at[quarter])
    fetch(down_parts[3], down_buf.at[3, :, pl.ds(0, half)])
    fetch(down_parts[4], down_buf.at[3, :, pl.ds(half, half)])

    acts = []
    for quarter in range(4):
        gate_act = up_act = None
        for part in range(PARTS):
            index = 2 * (quarter * PARTS + part)
            moves[index].wait()
            moves[index + 1].wait()
            rows = rows_ref[part]
            gate_term = jnp.dot(rows, gate_buf[quarter, part], preferred_element_type=jnp.float32)
            up_term = jnp.dot(rows, up_buf[quarter, part], preferred_element_type=jnp.float32)
            gate_act = gate_term if part == 0 else gate_act + gate_term
            up_act = up_term if part == 0 else up_act + up_term
        acts.append((gate_act / (1.0 + jnp.exp(-gate_act)) * up_act).astype(jnp.bfloat16))
    for move in moves[8 * PARTS :]:
        move.wait()
    for part in range(PARTS):
        total = None
        for quarter in range(4):
            term = jnp.dot(
                acts[quarter],
                down_buf[quarter, :, part * depth : (part + 1) * depth],
                preferred_element_type=jnp.float32,
            )
            total = term if quarter == 0 else total + term
        out_ref[part] = total.astype(jnp.bfloat16)


def run_expert(order, rows, gate_up_pieces, down_pieces):
    parts, slot_count, depth = rows.shape
    hidden_width = gate_up_pieces[0].shape[1]
    anywhere = pl.BlockSpec(memory_space=pl.ANY)
    operands = [*gate_up_pieces, *down_pieces]
    return pl.pallas_call(
        expert_kernel,
        in_specs=[
            pl.BlockSpec(memory_space=pltpu.SMEM),
            pl.BlockSpec(memory_space=pltpu.VMEM),
            *[anywhere] * len(operands),
        ],
        out_specs=pl.BlockSpec(memory_space=pltpu.VMEM),
        out_shape=jax.ShapeDtypeStruct((parts, slot_count, depth), jnp.bfloat16),
        scratch_shapes=[
            pltpu.VMEM((4, parts, depth, hidden_width), jnp.bfloat16),
            pltpu.VMEM((4, parts, depth, hidden_width), jnp.bfloat16),
            pltpu.VMEM((4, hidden_width, parts * depth), jnp.bfloat16),
            pltpu.SemaphoreType.DMA((8 * parts + 5,)),
        ],
        compiler_params=pltpu.CompilerParams(vmem_limit_bytes=56 * 1024 * 1024),
        name="expert",
    )(order, rows, *operands)


def body(
    queries,
    key_heads,
    value_heads,
    residual,
    out_weight,
    norm_gain,
    gate_weight,
    up_weight,
    down_weight,
    expert_ids,
    route_gates,
):
    tokens, model_width = residual.shape
    seq_size = lax.axis_size("seq")
    exp_size = lax.axis_size("exp")
    depth = model_width // PARTS
    fanout = expert_ids.shape[1]
    capacity = min(tokens, 3 * tokens * fanout // (2 * exp_size))
    slot_count = exp_size * capacity
    sent_count = PARTS * slot_count

    cand = lax.axis_index("cand")
    order = jnp.stack([cand, (cand + 3) % PARTS, (cand + 1) % PARTS, (cand + 2) % PARTS])
    own_piece = jnp.concatenate(
        [
            lax.dynamic_slice_in_dim(weight[0], cand * depth, depth, axis=0)
            for weight in (gate_weight, up_weight)
        ],
        axis=0,
    )
    before = shift(own_piece, "seq", 1)
    after = shift(own_piece, "seq", -1)

    pairs = jnp.concatenate(
        [
            key_heads.reshape(tokens, seq_size, HEAD_DIM),
            value_heads.reshape(tokens, seq_size, HEAD_DIM),
        ],
        axis=2,
    ).reshape(tokens, seq_size * 2 * HEAD_DIM)
    pair_local = lax.all_to_all(pairs, "seq", split_axis=1, concat_axis=0, tiled=True)
    pair_local = pair_local.reshape(seq_size, tokens, 2 * HEAD_DIM)
    query_rows = lax.all_to_all(queries, ("seq", "exp"), split_axis=1, concat_axis=0, tiled=True)
    pair_rows = lax.all_gather(pair_local, "exp", axis=1, tiled=True).reshape(
        seq_size * exp_size * tokens, 2 * HEAD_DIM
    )
    weight_rows = lax.all_gather(out_weight, "seq", axis=0, tiled=True)
    query_rows, before, after = meet(query_rows, before, after)
    far_gate = shift(before[:depth], "seq", 1)
    far_up = shift(after[depth:], "seq", -1)
    before_left, before_right = shift(before, "cand", 1), shift(before, "cand", -1)
    attended = attend(query_rows, pair_rows)
    attended, far_gate, far_up, before_left, before_right, after = meet(
        attended, far_gate, far_up, before_left, before_right, after
    )
    far = jnp.concatenate([far_gate, far_up], axis=0)
    after_left, after_right = shift(after, "cand", 1), shift(after, "cand", -1)
    head_cols = lax.all_to_all(attended, "seq", split_axis=0, concat_axis=1, tiled=True)
    head_cols, after_left, after_right, far = meet(head_cols, after_left, after_right, far)
    down_own = down_weight[0]
    down_before = shift(down_own, "seq", 1)
    down_after = shift(down_own, "seq", -1)
    before_far = shift(before_left, "cand", 1)
    far_left, far_right = shift(far, "cand", 1), shift(far, "cand", -1)
    projected = lax.psum_scatter(
        jnp.dot(head_cols, weight_rows, preferred_element_type=jnp.float32).astype(jnp.bfloat16),
        "exp",
        scatter_dimension=0,
        tiled=True,
    )
    projected, down_before, down_after, before_far, far_left, far_right, after_right = meet(
        projected, down_before, down_after, before_far, far_left, far_right, after_right
    )
    after_far = shift(after_right, "cand", -1)
    gate_far = shift(far_left[:depth], "cand", 1)
    up_far = shift(far_right[depth:], "cand", -1)
    half_width = model_width // 2
    down_far = [
        shift(down_before[:, :half_width], "seq", 1),
        shift(down_after[:, half_width:], "seq", -1),
    ]
    hidden = residual.astype(jnp.float32) + projected.astype(jnp.float32)
    mean_square = jnp.mean(hidden * hidden, axis=1, keepdims=True)
    normed = (hidden * lax.rsqrt(mean_square + norm_eps) * norm_gain.astype(jnp.float32)).astype(
        jnp.bfloat16
    )

    targets = slot_targets(expert_ids, capacity)
    token_pairs = jnp.tile(targets, (PARTS, 1))
    gate_pairs = jnp.tile(route_gates, (PARTS, 1))
    pair_part = lax.broadcasted_iota(jnp.int32, (sent_count, PARTS * tokens), 1) // tokens
    slot_of, part_of = sent_rows((sent_count, PARTS * tokens), 0, capacity)
    named = [token_pairs[:, k][None, :] == slot_of for k in range(fanout)]
    turn = jnp.where(part_of == 1, 3, jnp.where(part_of == 2, 1, jnp.where(part_of == 3, 2, 0)))
    turned = (cand + turn) % PARTS
    send_map = sum((name & (turned == pair_part)).astype(jnp.float32) for name in named).astype(
        jnp.bfloat16
    )
    blend_map = sum(
        jnp.where(name & (part_of == pair_part), gate_pairs[:, k][None, :], 0.0)
        for k, name in enumerate(named)
    )
    blend_high = blend_map.astype(jnp.bfloat16)
    blend_low = (blend_map - blend_high.astype(jnp.float32)).astype(jnp.bfloat16)
    row_slot, row_part = sent_rows((sent_count, sent_count), 1, capacity)
    plain_row = lax.broadcasted_iota(jnp.int32, (sent_count, sent_count), 0)
    order_map = (plain_row == row_part * slot_count + row_slot).astype(jnp.bfloat16)

    stacked = jnp.concatenate(
        [normed[:, part * depth : (part + 1) * depth] for part in range(PARTS)], axis=0
    )
    outgoing = jnp.dot(send_map, stacked, preferred_element_type=jnp.float32).astype(jnp.bfloat16)
    arrived = lax.all_to_all(outgoing, "exp", split_axis=0, concat_axis=0, tiled=True)
    ordered = jnp.dot(order_map, arrived, preferred_element_type=jnp.float32).astype(jnp.bfloat16)
    expert_out = run_expert(
        order,
        ordered.reshape(PARTS, slot_count, depth),
        [
            *(gate_weight[0], up_weight[0]),
            *(before, before_left, before_right, before_far),
            *(after, after_left, after_right, after_far),
            *(far, far_left, far_right, gate_far, up_far),
        ],
        [down_own, down_before, down_after, *down_far],
    )
    leaving = lax.dot_general(
        order_map,
        expert_out.reshape(sent_count, depth),
        (((0,), (0,)), ((), ())),
        preferred_element_type=jnp.float32,
    ).astype(jnp.bfloat16)
    returned = lax.all_to_all(leaving, "exp", split_axis=0, concat_axis=0, tiled=True)
    blended = sum(
        lax.dot_general(part, returned, (((0,), (0,)), ((), ())), preferred_element_type=jnp.float32)
        for part in (blend_high, blend_low)
    )
    blended = jnp.concatenate(
        [blended[part * tokens : (part + 1) * tokens] for part in range(PARTS)], axis=1
    )
    return (hidden + blended).astype(jnp.bfloat16)


def solution(mesh):
    placed = (
        P(("cand", "seq", "exp"), None),
        P(("cand", "seq", "exp"), None),
        P(("cand", "seq", "exp"), None),
        P(("cand", "seq", "exp"), None),
        P(("seq", "exp"), None),
        P(),
        P("exp", None, "seq"),
        P("exp", None, "seq"),
        P("exp", "seq", None),
        P(("cand", "seq", "exp"), None),
        P(("cand", "seq", "exp"), None),
    )
    return jax.shard_map(
        body, mesh=mesh, in_specs=placed, out_specs=P(("cand", "seq", "exp"), None), check_vma=False
    )
```

```python
import functools
import math

import jax
import jax.numpy as jnp
from jax import lax
from jax.experimental import pallas as pl
from jax.experimental.pallas import tpu as pltpu
from jax.sharding import PartitionSpec as P

HEAD_DIM = 128
BLOCK = 512
PARTS = 4

norm_eps = 1e-06


def attention_kernel(first_block, query_ref, pair_ref, *refs):
    out_ref = refs[-1]
    block = first_block + pl.program_id(0)
    rows = query_ref.shape[0]
    part = rows // 2
    factor = math.log2(math.e) / HEAD_DIM**0.5
    parts = [query_ref[index * part : (index + 1) * part, :] for index in range(2)]

    def scores_of(start, queries):
        keys = pair_ref[pl.ds(start, rows), :HEAD_DIM]
        return lax.dot_general(
            keys, queries, (((1,), (1,)), ((), ())), preferred_element_type=jnp.float32
        )

    def mix(start, shares):
        values = pair_ref[pl.ds(start, rows), HEAD_DIM:]
        return lax.dot_general(
            values, shares, (((0,), (0,)), ((), ())), preferred_element_type=jnp.float32
        )

    first = pl.multiple_of(block * rows, rows)
    carry = []
    for index in range(2):
        scores = scores_of(first, parts[index])
        key_pos = lax.broadcasted_iota(jnp.int32, (rows, part), 0)
        query_pos = index * part + lax.broadcasted_iota(jnp.int32, (rows, part), 1)
        scores = jnp.where(key_pos <= query_pos, scores, -1e30)
        top = jnp.max(scores, axis=0, keepdims=True)
        weights = jnp.exp2(scores * factor - top * factor)
        total = jnp.sum(weights, axis=0, keepdims=True)
        carry += [top, total, mix(first, weights.astype(jnp.bfloat16))]

    def step(turn, carry):
        start = pl.multiple_of(turn * rows, rows)
        after = []
        scores_both = [scores_of(start, parts[index]) for index in range(2)]
        for index in range(2):
            top, total, mixed = carry[3 * index : 3 * index + 3]
            scores = scores_both[index]
            new_top = jnp.maximum(top, jnp.max(scores, axis=0, keepdims=True))
            weights = jnp.exp2(scores * factor - new_top * factor)
            shrink = jnp.exp2((top - new_top) * factor)
            after += [
                new_top,
                total * shrink + jnp.sum(weights, axis=0, keepdims=True),
                mixed * shrink + mix(start, weights.astype(jnp.bfloat16)),
            ]
        return tuple(after)

    carry = lax.fori_loop(0, block, step, tuple(carry))
    for index in range(2):
        top, total, mixed = carry[3 * index : 3 * index + 3]
        out_ref[index * part : (index + 1) * part, :] = (
            (mixed * (1.0 / total)).T.astype(jnp.bfloat16)
        )


def attend(query_rows, pair_rows, first_block, last_block, so_far=None):
    seq_len = query_rows.shape[0]
    rows_spec = pl.BlockSpec((BLOCK, HEAD_DIM), lambda index: (first_block + index, 0))
    extra = [] if so_far is None else [so_far]
    return pl.pallas_call(
        functools.partial(attention_kernel, first_block),
        grid=(last_block - first_block,),
        in_specs=[
            rows_spec,
            pl.BlockSpec((seq_len, 2 * HEAD_DIM), lambda index: (0, 0)),
            *[pl.BlockSpec(memory_space=pl.ANY) for _ in extra],
        ],
        out_specs=rows_spec,
        out_shape=jax.ShapeDtypeStruct((seq_len, HEAD_DIM), jnp.bfloat16),
        input_output_aliases={2: 0} if extra else {},
        compiler_params=pltpu.CompilerParams(vmem_limit_bytes=40 * 1024 * 1024),
        name="attention",
    )(query_rows, pair_rows, *extra)


def slot_targets(expert_ids, capacity):
    tokens, fanout = expert_ids.shape
    entries = tokens * fanout
    flat_ids = expert_ids.reshape(entries)
    same_expert = flat_ids[:, None] == flat_ids[None, :]
    earlier = lax.broadcasted_iota(jnp.int32, (entries, entries), 1) < lax.broadcasted_iota(
        jnp.int32, (entries, entries), 0
    )
    slot_rank = jnp.sum((same_expert & earlier).astype(jnp.int32), axis=1)
    return (flat_ids * capacity + slot_rank).reshape(tokens, fanout)


def sent_rows(shape, dim, capacity):
    row = lax.broadcasted_iota(jnp.int32, shape, dim)
    within = row % (PARTS * capacity)
    return row // (PARTS * capacity) * capacity + within % capacity, within // capacity


def shift(array, axis, distance):
    size = lax.axis_size(axis)
    return lax.ppermute(array, axis, [(i, (i + distance) % size) for i in range(size)])


def pass_kernel(*refs):
    del refs


def meet(*arrays):
    anywhere = pl.BlockSpec(memory_space=pl.ANY)
    return pl.pallas_call(
        pass_kernel,
        in_specs=[anywhere] * len(arrays),
        out_specs=[anywhere] * len(arrays),
        out_shape=[jax.ShapeDtypeStruct(array.shape, array.dtype) for array in arrays],
        input_output_aliases={index: index for index in range(len(arrays))},
        name="meet",
    )(*arrays)


def expert_kernel(order_ref, rows_ref, *refs):
    gate_own, up_own = refs[:2]
    near = refs[2:8]
    first_sets, second_sets = refs[8:10], refs[10:12]
    before_opposite, gate_after_opposite, gate_far_opposite, second_opposite = refs[12:16]
    down_parts = refs[16:21]
    out_ref, gate_buf, up_buf, down_buf, sems = refs[21:]
    depth = rows_ref.shape[2]
    half = down_buf.shape[2] // 2
    moves = []

    def fetch(source, target):
        move = pltpu.make_async_copy(source, target, sems.at[len(moves)])
        move.start()
        moves.append(move)

    def rows_of(ref, index):
        return ref.at[pl.ds(index * depth, depth)]

    starts = [pl.multiple_of(order_ref[part] * depth, depth) for part in range(PARTS)]
    gates = [[gate_own.at[pl.ds(start, depth)] for start in starts]]
    ups = [[up_own.at[pl.ds(start, depth)] for start in starts]]
    gates.append([near[0], *[rows_of(ref, 0) for ref in (*first_sets, before_opposite)]])
    ups.append([near[1], *[rows_of(ref, 1) for ref in (*first_sets, before_opposite)]])
    gates.append([near[2], *[rows_of(ref, 2) for ref in first_sets], gate_after_opposite])
    ups.append([near[3], *[rows_of(ref, 1) for ref in second_sets], rows_of(second_opposite, 0)])
    gates.append([near[4], *[rows_of(ref, 0) for ref in second_sets], gate_far_opposite])
    ups.append([near[5], *[rows_of(ref, 2) for ref in second_sets], rows_of(second_opposite, 1)])
    for quarter in range(4):
        for part in range(PARTS):
            fetch(gates[quarter][part], gate_buf.at[quarter, part])
            fetch(ups[quarter][part], up_buf.at[quarter, part])
    for quarter in range(3):
        fetch(down_parts[quarter], down_buf.at[quarter])
    fetch(down_parts[3], down_buf.at[3, :, pl.ds(0, half)])
    fetch(down_parts[4], down_buf.at[3, :, pl.ds(half, half)])

    acts = []
    for quarter in range(4):
        gate_act = up_act = None
        for part in range(PARTS):
            index = 2 * (quarter * PARTS + part)
            moves[index].wait()
            moves[index + 1].wait()
            rows = rows_ref[part]
            gate_term = jnp.dot(rows, gate_buf[quarter, part], preferred_element_type=jnp.float32)
            up_term = jnp.dot(rows, up_buf[quarter, part], preferred_element_type=jnp.float32)
            gate_act = gate_term if part == 0 else gate_act + gate_term
            up_act = up_term if part == 0 else up_act + up_term
        acts.append((gate_act / (1.0 + jnp.exp(-gate_act)) * up_act).astype(jnp.bfloat16))
    for move in moves[8 * PARTS :]:
        move.wait()
    for part in range(PARTS):
        total = None
        for quarter in range(4):
            term = jnp.dot(
                acts[quarter],
                down_buf[quarter, :, part * depth : (part + 1) * depth],
                preferred_element_type=jnp.float32,
            )
            total = term if quarter == 0 else total + term
        out_ref[part] = total.astype(jnp.bfloat16)


def run_expert(order, rows, gate_up_pieces, down_pieces):
    parts, slot_count, depth = rows.shape
    hidden_width = gate_up_pieces[0].shape[1]
    anywhere = pl.BlockSpec(memory_space=pl.ANY)
    operands = [*gate_up_pieces, *down_pieces]
    return pl.pallas_call(
        expert_kernel,
        in_specs=[
            pl.BlockSpec(memory_space=pltpu.SMEM),
            pl.BlockSpec(memory_space=pltpu.VMEM),
            *[anywhere] * len(operands),
        ],
        out_specs=pl.BlockSpec(memory_space=pltpu.VMEM),
        out_shape=jax.ShapeDtypeStruct((parts, slot_count, depth), jnp.bfloat16),
        scratch_shapes=[
            pltpu.VMEM((4, parts, depth, hidden_width), jnp.bfloat16),
            pltpu.VMEM((4, parts, depth, hidden_width), jnp.bfloat16),
            pltpu.VMEM((4, hidden_width, parts * depth), jnp.bfloat16),
            pltpu.SemaphoreType.DMA((8 * parts + 5,)),
        ],
        compiler_params=pltpu.CompilerParams(vmem_limit_bytes=56 * 1024 * 1024),
        name="expert",
    )(order, rows, *operands)


def body(
    queries,
    key_heads,
    value_heads,
    residual,
    out_weight,
    norm_gain,
    gate_weight,
    up_weight,
    down_weight,
    expert_ids,
    route_gates,
):
    tokens, model_width = residual.shape
    seq_size = lax.axis_size("seq")
    exp_size = lax.axis_size("exp")
    depth = model_width // PARTS
    fanout = expert_ids.shape[1]
    capacity = min(tokens, 3 * tokens * fanout // (2 * exp_size))
    slot_count = exp_size * capacity
    sent_count = PARTS * slot_count

    cand = lax.axis_index("cand")
    order = jnp.stack([cand, (cand + 3) % PARTS, (cand + 1) % PARTS, (cand + 2) % PARTS])
    own_gate, own_up = (
        lax.dynamic_slice_in_dim(weight[0], cand * depth, depth, axis=0)
        for weight in (gate_weight, up_weight)
    )
    gate_before, gate_after = shift(own_gate, "seq", 1), shift(own_gate, "seq", -1)
    up_before, up_after = shift(own_up, "seq", 1), shift(own_up, "seq", -1)

    pairs = jnp.concatenate(
        [
            key_heads.reshape(tokens, seq_size, HEAD_DIM),
            value_heads.reshape(tokens, seq_size, HEAD_DIM),
        ],
        axis=2,
    ).reshape(tokens, seq_size * 2 * HEAD_DIM)
    pair_local = lax.all_to_all(pairs, "seq", split_axis=1, concat_axis=0, tiled=True)
    pair_local = pair_local.reshape(seq_size, tokens, 2 * HEAD_DIM)
    query_rows = lax.all_to_all(queries, ("seq", "exp"), split_axis=1, concat_axis=0, tiled=True)
    pair_rows = lax.all_gather(pair_local, "exp", axis=1, tiled=True).reshape(
        seq_size * exp_size * tokens, 2 * HEAD_DIM
    )
    weight_rows = lax.all_gather(out_weight, "seq", axis=0, tiled=True)
    blocks = query_rows.shape[0] // BLOCK
    split_block = blocks * 3 // 4
    attended = attend(query_rows, pair_rows, 0, split_block)
    attended, gate_before, up_before, gate_after, up_after = meet(
        attended, gate_before, up_before, gate_after, up_after
    )
    gate_far = shift(gate_before, "seq", 1)
    up_far = shift(up_after, "seq", -1)
    first_set = jnp.concatenate([gate_before, up_before, gate_after], axis=0)
    first_left, first_right = shift(first_set, "cand", 1), shift(first_set, "cand", -1)
    attended = attend(query_rows, pair_rows, split_block, blocks, attended)
    attended, gate_far, up_far = meet(attended, gate_far, up_far)
    head_cols = lax.all_to_all(attended, "seq", split_axis=0, concat_axis=1, tiled=True)
    product = jnp.dot(head_cols, weight_rows, preferred_element_type=jnp.float32).astype(
        jnp.bfloat16
    )
    product, first_left, first_right = meet(product, first_left, first_right)
    down_own = down_weight[0]
    down_before = shift(down_own, "seq", 1)
    down_after = shift(down_own, "seq", -1)
    second_set = jnp.concatenate([gate_far, up_after, up_far], axis=0)
    second_left, second_right = shift(second_set, "cand", 1), shift(second_set, "cand", -1)
    before_opposite = shift(first_left[: 2 * depth], "cand", 1)
    projected = lax.psum_scatter(product, "exp", scatter_dimension=0, tiled=True)
    (
        projected,
        first_right,
        second_left,
        second_right,
        down_before,
        down_after,
        before_opposite,
    ) = meet(
        projected,
        first_right,
        second_left,
        second_right,
        down_before,
        down_after,
        before_opposite,
    )
    gate_after_opposite = shift(first_right[2 * depth :], "cand", -1)
    gate_far_opposite = shift(second_left[:depth], "cand", 1)
    second_opposite = shift(second_right[depth:], "cand", -1)
    half_width = model_width // 2
    down_far = [
        shift(down_before[:, :half_width], "seq", 1),
        shift(down_after[:, half_width:], "seq", -1),
    ]
    hidden = residual.astype(jnp.float32) + projected.astype(jnp.float32)
    mean_square = jnp.mean(hidden * hidden, axis=1, keepdims=True)
    normed = (hidden * lax.rsqrt(mean_square + norm_eps) * norm_gain.astype(jnp.float32)).astype(
        jnp.bfloat16
    )

    targets = slot_targets(expert_ids, capacity)
    token_pairs = jnp.tile(targets, (PARTS, 1))
    gate_pairs = jnp.tile(route_gates, (PARTS, 1))
    pair_part = lax.broadcasted_iota(jnp.int32, (sent_count, PARTS * tokens), 1) // tokens
    slot_of, part_of = sent_rows((sent_count, PARTS * tokens), 0, capacity)
    named = [token_pairs[:, k][None, :] == slot_of for k in range(fanout)]
    turn = jnp.where(part_of == 1, 3, jnp.where(part_of == 2, 1, jnp.where(part_of == 3, 2, 0)))
    turned = (cand + turn) % PARTS
    send_map = sum((name & (turned == pair_part)).astype(jnp.float32) for name in named).astype(
        jnp.bfloat16
    )
    blend_map = sum(
        jnp.where(name & (part_of == pair_part), gate_pairs[:, k][None, :], 0.0)
        for k, name in enumerate(named)
    )
    blend_high = blend_map.astype(jnp.bfloat16)
    blend_low = (blend_map - blend_high.astype(jnp.float32)).astype(jnp.bfloat16)
    row_slot, row_part = sent_rows((sent_count, sent_count), 1, capacity)
    plain_row = lax.broadcasted_iota(jnp.int32, (sent_count, sent_count), 0)
    order_map = (plain_row == row_part * slot_count + row_slot).astype(jnp.bfloat16)

    stacked = jnp.concatenate(
        [normed[:, part * depth : (part + 1) * depth] for part in range(PARTS)], axis=0
    )
    outgoing = jnp.dot(send_map, stacked, preferred_element_type=jnp.float32).astype(jnp.bfloat16)
    arrived = lax.all_to_all(outgoing, "exp", split_axis=0, concat_axis=0, tiled=True)
    ordered = jnp.dot(order_map, arrived, preferred_element_type=jnp.float32).astype(jnp.bfloat16)
    expert_out = run_expert(
        order,
        ordered.reshape(PARTS, slot_count, depth),
        [
            *(gate_weight[0], up_weight[0]),
            *(gate_before, up_before, gate_after, up_after, gate_far, up_far),
            *(first_left, first_right, second_left, second_right),
            *(before_opposite, gate_after_opposite, gate_far_opposite, second_opposite),
        ],
        [down_own, down_before, down_after, *down_far],
    )
    leaving = lax.dot_general(
        order_map,
        expert_out.reshape(sent_count, depth),
        (((0,), (0,)), ((), ())),
        preferred_element_type=jnp.float32,
    ).astype(jnp.bfloat16)
    returned = lax.all_to_all(leaving, "exp", split_axis=0, concat_axis=0, tiled=True)
    blended = sum(
        lax.dot_general(part, returned, (((0,), (0,)), ((), ())), preferred_element_type=jnp.float32)
        for part in (blend_high, blend_low)
    )
    blended = jnp.concatenate(
        [blended[part * tokens : (part + 1) * tokens] for part in range(PARTS)], axis=1
    )
    return (hidden + blended).astype(jnp.bfloat16)


def solution(mesh):
    placed = (
        P(("cand", "seq", "exp"), None),
        P(("cand", "seq", "exp"), None),
        P(("cand", "seq", "exp"), None),
        P(("cand", "seq", "exp"), None),
        P(("seq", "exp"), None),
        P(),
        P("exp", None, "seq"),
        P("exp", None, "seq"),
        P("exp", "seq", None),
        P(("cand", "seq", "exp"), None),
        P(("cand", "seq", "exp"), None),
    )
    return jax.shard_map(
        body, mesh=mesh, in_specs=placed, out_specs=P(("cand", "seq", "exp"), None), check_vma=False
    )
```

```python
import math

import jax
import jax.numpy as jnp
from jax import lax
from jax.experimental import pallas as pl
from jax.experimental.pallas import tpu as pltpu
from jax.sharding import PartitionSpec as P

HEAD_DIM = 128
BLOCK = 512
PARTS = 4

norm_eps = 1e-06


def attention_kernel(query_ref, pair_ref, out_ref):
    factor = math.log2(math.e) / HEAD_DIM**0.5
    for start in range(0, query_ref.shape[0], BLOCK):
        seen = start + BLOCK
        scores = lax.dot_general(
            pair_ref[:seen, :HEAD_DIM],
            query_ref[start:seen, :],
            (((1,), (1,)), ((), ())),
            preferred_element_type=jnp.float32,
        )
        key_pos = lax.broadcasted_iota(jnp.int32, scores.shape, 0)
        query_pos = start + lax.broadcasted_iota(jnp.int32, scores.shape, 1)
        scores = jnp.where(key_pos <= query_pos, scores, -1e30)
        top = jnp.max(scores, axis=0, keepdims=True)
        weights = jnp.exp2(scores * factor - top * factor)
        total = jnp.sum(weights, axis=0, keepdims=True)
        mixed = lax.dot_general(
            pair_ref[:seen, HEAD_DIM:],
            weights.astype(jnp.bfloat16),
            (((0,), (0,)), ((), ())),
            preferred_element_type=jnp.float32,
        )
        out_ref[start:seen, :] = (mixed * (1.0 / total)).T.astype(jnp.bfloat16)


def attend(query_rows, pair_rows):
    whole = pl.BlockSpec(memory_space=pltpu.VMEM)
    return pl.pallas_call(
        attention_kernel,
        in_specs=[whole, whole],
        out_specs=whole,
        out_shape=jax.ShapeDtypeStruct(query_rows.shape, jnp.bfloat16),
        compiler_params=pltpu.CompilerParams(vmem_limit_bytes=48 * 1024 * 1024),
        name="attention",
    )(query_rows, pair_rows)


def slot_targets(expert_ids, capacity):
    tokens, fanout = expert_ids.shape
    entries = tokens * fanout
    flat_ids = expert_ids.reshape(entries)
    same_expert = flat_ids[:, None] == flat_ids[None, :]
    earlier = lax.broadcasted_iota(jnp.int32, (entries, entries), 1) < lax.broadcasted_iota(
        jnp.int32, (entries, entries), 0
    )
    slot_rank = jnp.sum((same_expert & earlier).astype(jnp.int32), axis=1)
    return (flat_ids * capacity + slot_rank).reshape(tokens, fanout)


def sent_rows(shape, dim, capacity):
    row = lax.broadcasted_iota(jnp.int32, shape, dim)
    within = row % (PARTS * capacity)
    return row // (PARTS * capacity) * capacity + within % capacity, within // capacity


def shift(array, axis, distance):
    size = lax.axis_size(axis)
    return lax.ppermute(array, axis, [(i, (i + distance) % size) for i in range(size)])


def pass_kernel(*refs):
    del refs


def meet(*arrays):
    anywhere = pl.BlockSpec(memory_space=pl.ANY)
    return pl.pallas_call(
        pass_kernel,
        in_specs=[anywhere] * len(arrays),
        out_specs=[anywhere] * len(arrays),
        out_shape=[jax.ShapeDtypeStruct(array.shape, array.dtype) for array in arrays],
        input_output_aliases={index: index for index in range(len(arrays))},
        name="meet",
    )(*arrays)


def expert_kernel(order_ref, rows_ref, *refs):
    gate_own, up_own = refs[:2]
    near = refs[2:8]
    first_sets, second_sets = refs[8:10], refs[10:12]
    before_opposite, gate_after_opposite, gate_far_opposite, second_opposite = refs[12:16]
    down_parts = refs[16:21]
    out_ref, gate_buf, up_buf, down_buf, sems = refs[21:]
    depth = rows_ref.shape[2]
    half = down_buf.shape[2] // 2
    moves = []

    def fetch(source, target):
        move = pltpu.make_async_copy(source, target, sems.at[len(moves)])
        move.start()
        moves.append(move)

    def rows_of(ref, index):
        return ref.at[pl.ds(index * depth, depth)]

    starts = [pl.multiple_of(order_ref[part] * depth, depth) for part in range(PARTS)]
    gates = [[gate_own.at[pl.ds(start, depth)] for start in starts]]
    ups = [[up_own.at[pl.ds(start, depth)] for start in starts]]
    gates.append([near[0], *[rows_of(ref, 0) for ref in (*first_sets, before_opposite)]])
    ups.append([near[1], *[rows_of(ref, 1) for ref in (*first_sets, before_opposite)]])
    gates.append([near[2], *[rows_of(ref, 2) for ref in first_sets], gate_after_opposite])
    ups.append([near[3], *[rows_of(ref, 1) for ref in second_sets], rows_of(second_opposite, 0)])
    gates.append([near[4], *[rows_of(ref, 0) for ref in second_sets], gate_far_opposite])
    ups.append([near[5], *[rows_of(ref, 2) for ref in second_sets], rows_of(second_opposite, 1)])
    for quarter in range(4):
        for part in range(PARTS):
            fetch(gates[quarter][part], gate_buf.at[quarter, part])
            fetch(ups[quarter][part], up_buf.at[quarter, part])
    for quarter in range(3):
        fetch(down_parts[quarter], down_buf.at[quarter])
    fetch(down_parts[3], down_buf.at[3, :, pl.ds(0, half)])
    fetch(down_parts[4], down_buf.at[3, :, pl.ds(half, half)])

    acts = []
    for quarter in range(4):
        gate_act = up_act = None
        for part in range(PARTS):
            index = 2 * (quarter * PARTS + part)
            moves[index].wait()
            moves[index + 1].wait()
            rows = rows_ref[part]
            gate_term = jnp.dot(rows, gate_buf[quarter, part], preferred_element_type=jnp.float32)
            up_term = jnp.dot(rows, up_buf[quarter, part], preferred_element_type=jnp.float32)
            gate_act = gate_term if part == 0 else gate_act + gate_term
            up_act = up_term if part == 0 else up_act + up_term
        acts.append((gate_act / (1.0 + jnp.exp(-gate_act)) * up_act).astype(jnp.bfloat16))
    for move in moves[8 * PARTS :]:
        move.wait()
    for part in range(PARTS):
        total = None
        for quarter in range(4):
            term = jnp.dot(
                acts[quarter],
                down_buf[quarter, :, part * depth : (part + 1) * depth],
                preferred_element_type=jnp.float32,
            )
            total = term if quarter == 0 else total + term
        out_ref[part] = total.astype(jnp.bfloat16)


def run_expert(order, rows, gate_up_pieces, down_pieces):
    parts, slot_count, depth = rows.shape
    hidden_width = gate_up_pieces[0].shape[1]
    anywhere = pl.BlockSpec(memory_space=pl.ANY)
    operands = [*gate_up_pieces, *down_pieces]
    return pl.pallas_call(
        expert_kernel,
        in_specs=[
            pl.BlockSpec(memory_space=pltpu.SMEM),
            pl.BlockSpec(memory_space=pltpu.VMEM),
            *[anywhere] * len(operands),
        ],
        out_specs=pl.BlockSpec(memory_space=pltpu.VMEM),
        out_shape=jax.ShapeDtypeStruct((parts, slot_count, depth), jnp.bfloat16),
        scratch_shapes=[
            pltpu.VMEM((4, parts, depth, hidden_width), jnp.bfloat16),
            pltpu.VMEM((4, parts, depth, hidden_width), jnp.bfloat16),
            pltpu.VMEM((4, hidden_width, parts * depth), jnp.bfloat16),
            pltpu.SemaphoreType.DMA((8 * parts + 5,)),
        ],
        compiler_params=pltpu.CompilerParams(vmem_limit_bytes=56 * 1024 * 1024),
        name="expert",
    )(order, rows, *operands)


def body(
    queries,
    key_heads,
    value_heads,
    residual,
    out_weight,
    norm_gain,
    gate_weight,
    up_weight,
    down_weight,
    expert_ids,
    route_gates,
):
    tokens, model_width = residual.shape
    seq_size = lax.axis_size("seq")
    exp_size = lax.axis_size("exp")
    depth = model_width // PARTS
    fanout = expert_ids.shape[1]
    capacity = min(tokens, 3 * tokens * fanout // (2 * exp_size))
    slot_count = exp_size * capacity
    sent_count = PARTS * slot_count

    cand = lax.axis_index("cand")
    order = jnp.stack([cand, (cand + 3) % PARTS, (cand + 1) % PARTS, (cand + 2) % PARTS])
    own_gate, own_up = (
        lax.dynamic_slice_in_dim(weight[0], cand * depth, depth, axis=0)
        for weight in (gate_weight, up_weight)
    )
    gate_before, gate_after = shift(own_gate, "seq", 1), shift(own_gate, "seq", -1)
    up_before, up_after = shift(own_up, "seq", 1), shift(own_up, "seq", -1)

    pairs = jnp.concatenate(
        [
            key_heads.reshape(tokens, seq_size, HEAD_DIM),
            value_heads.reshape(tokens, seq_size, HEAD_DIM),
        ],
        axis=2,
    ).reshape(tokens, seq_size * 2 * HEAD_DIM)
    pair_local = lax.all_to_all(pairs, "seq", split_axis=1, concat_axis=0, tiled=True)
    pair_local = pair_local.reshape(seq_size, tokens, 2 * HEAD_DIM)
    query_rows = lax.all_to_all(queries, ("seq", "exp"), split_axis=1, concat_axis=0, tiled=True)
    pair_rows = lax.all_gather(pair_local, "exp", axis=1, tiled=True).reshape(
        seq_size * exp_size * tokens, 2 * HEAD_DIM
    )
    weight_rows = lax.all_gather(out_weight, "seq", axis=0, tiled=True)
    attended = attend(query_rows, pair_rows)
    attended, gate_before, up_before, gate_after, up_after = meet(
        attended, gate_before, up_before, gate_after, up_after
    )
    gate_far = shift(gate_before, "seq", 1)
    up_far = shift(up_after, "seq", -1)
    first_set = jnp.concatenate([gate_before, up_before, gate_after], axis=0)
    first_left, first_right = shift(first_set, "cand", 1), shift(first_set, "cand", -1)
    head_cols = lax.all_to_all(attended, "seq", split_axis=0, concat_axis=1, tiled=True)
    product = jnp.dot(head_cols, weight_rows, preferred_element_type=jnp.float32).astype(
        jnp.bfloat16
    )
    product, first_left, first_right, gate_far, up_far = meet(
        product, first_left, first_right, gate_far, up_far
    )
    down_own = down_weight[0]
    down_before = shift(down_own, "seq", 1)
    down_after = shift(down_own, "seq", -1)
    second_set = jnp.concatenate([gate_far, up_after, up_far], axis=0)
    second_left, second_right = shift(second_set, "cand", 1), shift(second_set, "cand", -1)
    gate_after_opposite = shift(first_right[2 * depth :], "cand", -1)
    projected = lax.psum_scatter(product, "exp", scatter_dimension=0, tiled=True)
    (
        projected,
        first_left,
        second_left,
        second_right,
        down_before,
        down_after,
        gate_after_opposite,
    ) = meet(
        projected,
        first_left,
        second_left,
        second_right,
        down_before,
        down_after,
        gate_after_opposite,
    )
    before_opposite = shift(first_left[: 2 * depth], "cand", 1)
    gate_far_opposite = shift(second_left[:depth], "cand", 1)
    second_opposite = shift(second_right[depth:], "cand", -1)
    half_width = model_width // 2
    down_far = [
        shift(down_before[:, :half_width], "seq", 1),
        shift(down_after[:, half_width:], "seq", -1),
    ]
    hidden = residual.astype(jnp.float32) + projected.astype(jnp.float32)
    mean_square = jnp.mean(hidden * hidden, axis=1, keepdims=True)
    normed = (hidden * lax.rsqrt(mean_square + norm_eps) * norm_gain.astype(jnp.float32)).astype(
        jnp.bfloat16
    )

    targets = slot_targets(expert_ids, capacity)
    token_pairs = jnp.tile(targets, (PARTS, 1))
    gate_pairs = jnp.tile(route_gates, (PARTS, 1))
    pair_part = lax.broadcasted_iota(jnp.int32, (sent_count, PARTS * tokens), 1) // tokens
    slot_of, part_of = sent_rows((sent_count, PARTS * tokens), 0, capacity)
    named = [token_pairs[:, k][None, :] == slot_of for k in range(fanout)]
    turn = jnp.where(part_of == 1, 3, jnp.where(part_of == 2, 1, jnp.where(part_of == 3, 2, 0)))
    turned = (cand + turn) % PARTS
    send_map = sum((name & (turned == pair_part)).astype(jnp.float32) for name in named).astype(
        jnp.bfloat16
    )
    blend_map = sum(
        jnp.where(name & (part_of == pair_part), gate_pairs[:, k][None, :], 0.0)
        for k, name in enumerate(named)
    )
    blend_high = blend_map.astype(jnp.bfloat16)
    blend_low = (blend_map - blend_high.astype(jnp.float32)).astype(jnp.bfloat16)
    row_slot, row_part = sent_rows((sent_count, sent_count), 1, capacity)
    plain_row = lax.broadcasted_iota(jnp.int32, (sent_count, sent_count), 0)
    order_map = (plain_row == row_part * slot_count + row_slot).astype(jnp.bfloat16)

    stacked = jnp.concatenate(
        [normed[:, part * depth : (part + 1) * depth] for part in range(PARTS)], axis=0
    )
    outgoing = jnp.dot(send_map, stacked, preferred_element_type=jnp.float32).astype(jnp.bfloat16)
    arrived = lax.all_to_all(outgoing, "exp", split_axis=0, concat_axis=0, tiled=True)
    ordered = jnp.dot(order_map, arrived, preferred_element_type=jnp.float32).astype(jnp.bfloat16)
    expert_out = run_expert(
        order,
        ordered.reshape(PARTS, slot_count, depth),
        [
            *(gate_weight[0], up_weight[0]),
            *(gate_before, up_before, gate_after, up_after, gate_far, up_far),
            *(first_left, first_right, second_left, second_right),
            *(before_opposite, gate_after_opposite, gate_far_opposite, second_opposite),
        ],
        [down_own, down_before, down_after, *down_far],
    )
    leaving = lax.dot_general(
        order_map,
        expert_out.reshape(sent_count, depth),
        (((0,), (0,)), ((), ())),
        preferred_element_type=jnp.float32,
    ).astype(jnp.bfloat16)
    returned = lax.all_to_all(leaving, "exp", split_axis=0, concat_axis=0, tiled=True)
    blended = sum(
        lax.dot_general(part, returned, (((0,), (0,)), ((), ())), preferred_element_type=jnp.float32)
        for part in (blend_high, blend_low)
    )
    blended = jnp.concatenate(
        [blended[part * tokens : (part + 1) * tokens] for part in range(PARTS)], axis=1
    )
    return (hidden + blended).astype(jnp.bfloat16)


def solution(mesh):
    placed = (
        P(("cand", "seq", "exp"), None),
        P(("cand", "seq", "exp"), None),
        P(("cand", "seq", "exp"), None),
        P(("cand", "seq", "exp"), None),
        P(("seq", "exp"), None),
        P(),
        P("exp", None, "seq"),
        P("exp", None, "seq"),
        P("exp", "seq", None),
        P(("cand", "seq", "exp"), None),
        P(("cand", "seq", "exp"), None),
    )
    return jax.shard_map(
        body, mesh=mesh, in_specs=placed, out_specs=P(("cand", "seq", "exp"), None), check_vma=False
    )
```

```python
import functools
import math

import jax
import jax.numpy as jnp
from jax import lax
from jax.experimental import pallas as pl
from jax.experimental.pallas import tpu as pltpu
from jax.sharding import PartitionSpec as P

HEAD_DIM = 128
BLOCK = 512
PARTS = 4

norm_eps = 1e-06


def attention_kernel(query_ref, pair_ref, out_ref):
    factor = math.log2(math.e) / HEAD_DIM**0.5
    for start in range(0, query_ref.shape[0], BLOCK):
        seen = start + BLOCK
        scores = lax.dot_general(
            pair_ref[:seen, :HEAD_DIM],
            query_ref[start:seen, :],
            (((1,), (1,)), ((), ())),
            preferred_element_type=jnp.float32,
        )
        key_pos = lax.broadcasted_iota(jnp.int32, scores.shape, 0)
        query_pos = start + lax.broadcasted_iota(jnp.int32, scores.shape, 1)
        scores = jnp.where(key_pos <= query_pos, scores, -1e30)
        top = jnp.max(scores, axis=0, keepdims=True)
        weights = jnp.exp2(scores * factor - top * factor)
        total = jnp.sum(weights, axis=0, keepdims=True)
        mixed = lax.dot_general(
            pair_ref[:seen, HEAD_DIM:],
            weights.astype(jnp.bfloat16),
            (((0,), (0,)), ((), ())),
            preferred_element_type=jnp.float32,
        )
        out_ref[start:seen, :] = (mixed * (1.0 / total)).T.astype(jnp.bfloat16)


def attend(query_rows, pair_rows):
    whole = pl.BlockSpec(memory_space=pltpu.VMEM)
    return pl.pallas_call(
        attention_kernel,
        in_specs=[whole, whole],
        out_specs=whole,
        out_shape=jax.ShapeDtypeStruct(query_rows.shape, jnp.bfloat16),
        compiler_params=pltpu.CompilerParams(vmem_limit_bytes=48 * 1024 * 1024),
        name="attention",
    )(query_rows, pair_rows)


def slot_targets(expert_ids, capacity):
    tokens, fanout = expert_ids.shape
    entries = tokens * fanout
    flat_ids = expert_ids.reshape(entries)
    same_expert = flat_ids[:, None] == flat_ids[None, :]
    earlier = lax.broadcasted_iota(jnp.int32, (entries, entries), 1) < lax.broadcasted_iota(
        jnp.int32, (entries, entries), 0
    )
    slot_rank = jnp.sum((same_expert & earlier).astype(jnp.int32), axis=1)
    return (flat_ids * capacity + slot_rank).reshape(tokens, fanout)


def sent_rows(shape, dim, capacity):
    row = lax.broadcasted_iota(jnp.int32, shape, dim)
    within = row % (PARTS * capacity)
    return row // (PARTS * capacity) * capacity + within % capacity, within // capacity


def shift(array, axis, distance):
    size = lax.axis_size(axis)
    return lax.ppermute(array, axis, [(i, (i + distance) % size) for i in range(size)])


def meet_kernel(count, cuts, *refs):
    held, copies, sems = refs[:count], refs[2 * count : -1], refs[-1]
    moves = []
    for target, cut in zip(copies, cuts):
        row = 0
        for source, start, rows in cut:
            move = pltpu.make_async_copy(
                held[source].at[pl.ds(start, rows)],
                target.at[pl.ds(row, rows)],
                sems.at[len(moves)],
            )
            move.start()
            moves.append(move)
            row += rows
    for move in moves:
        move.wait()


def meet(*arrays, cuts=()):
    anywhere = pl.BlockSpec(memory_space=pl.ANY)
    held = [jax.ShapeDtypeStruct(array.shape, array.dtype) for array in arrays]
    made = [
        jax.ShapeDtypeStruct(
            (sum(rows for _, _, rows in cut), arrays[cut[0][0]].shape[1]), arrays[cut[0][0]].dtype
        )
        for cut in cuts
    ]
    return pl.pallas_call(
        functools.partial(meet_kernel, len(arrays), cuts),
        in_specs=[anywhere] * len(arrays),
        out_specs=[anywhere] * (len(arrays) + len(made)),
        out_shape=held + made,
        input_output_aliases={index: index for index in range(len(arrays))},
        scratch_shapes=[pltpu.SemaphoreType.DMA((max(1, sum(len(cut) for cut in cuts)),))],
        name="meet",
    )(*arrays)


def project_kernel(order_ref, heads_ref, own_ref, others_ref, out_ref, buf, sems):
    step, last = pl.program_id(0), pl.num_programs(0) - 1
    width = buf.shape[2]
    slot = step % 2

    def leave(index, slot):
        start = pl.multiple_of(index * width, width)
        return pltpu.make_async_copy(buf.at[slot], out_ref.at[:, pl.ds(start, width)], sems.at[slot])

    @pl.when(step >= 2)
    def _():
        leave(step - 2, slot).wait()

    heads = jnp.concatenate([heads_ref[order_ref[index]] for index in range(4)], axis=1)
    weight = jnp.concatenate([own_ref[...], others_ref[...]], axis=0)
    buf[slot] = jnp.dot(heads, weight, preferred_element_type=jnp.float32).astype(jnp.bfloat16)
    leave(step, slot).start()

    @pl.when(step == last)
    def _():
        leave(step - 1, 1 - slot).wait()
        leave(step, slot).wait()


def project(order, head_rows, own_weight, other_weights):
    sources, tokens, head_dim = head_rows.shape
    width = other_weights.shape[1]
    blocks = own_weight.shape[1] // width
    others = (sources - 1) * head_dim
    return pl.pallas_call(
        project_kernel,
        grid=(blocks,),
        in_specs=[
            pl.BlockSpec(memory_space=pltpu.SMEM),
            pl.BlockSpec((sources, tokens, head_dim), lambda index: (0, 0, 0)),
            pl.BlockSpec((head_dim, width), lambda index: (0, index)),
            pl.BlockSpec((others, width), lambda index: (index, 0)),
        ],
        out_specs=pl.BlockSpec(memory_space=pltpu.HBM),
        out_shape=pltpu.HBM((tokens, blocks * width), jnp.bfloat16),
        scratch_shapes=[
            pltpu.VMEM((2, tokens, width), jnp.bfloat16),
            pltpu.SemaphoreType.DMA((2,)),
        ],
        compiler_params=pltpu.CompilerParams(vmem_limit_bytes=32 * 1024 * 1024),
        name="project",
    )(order, head_rows, own_weight, other_weights)


def widen_kernel(order_ref, rows_ref, *refs):
    gate_own, up_own, before, after, gate_far, up_far, left, right = refs[:8]
    gate_out, up_out, gate_buf, up_buf, sems = refs[8:]
    depth = rows_ref.shape[2]

    def rows_of(ref, index):
        return ref.at[pl.ds(index * depth, depth)]

    starts = [pl.multiple_of(order_ref[part] * depth, depth) for part in range(PARTS)]
    sets = (left, right)
    pairs = [
        [(gate_own.at[pl.ds(start, depth)], up_own.at[pl.ds(start, depth)]) for start in starts],
        [(rows_of(ref, 0), rows_of(ref, 1)) for ref in (before, *sets)],
        [(rows_of(after, 0), rows_of(after, 1))]
        + [(rows_of(ref, 4), rows_of(ref, 5)) for ref in sets],
        [(gate_far, up_far)] + [(rows_of(ref, 2), rows_of(ref, 3)) for ref in sets],
    ]
    moves = []
    for quarter, parts in enumerate(pairs):
        for part, sources in enumerate(parts):
            for source, target in zip(sources, (gate_buf, up_buf)):
                move = pltpu.make_async_copy(source, target.at[quarter, part], sems.at[len(moves)])
                move.start()
                moves.append(move)
    waiting = iter(moves)
    for quarter, parts in enumerate(pairs):
        sums = [None, None]
        for part in range(len(parts)):
            for index, buf in enumerate((gate_buf, up_buf)):
                next(waiting).wait()
                term = jnp.dot(
                    rows_ref[part], buf[quarter, part], preferred_element_type=jnp.float32
                )
                sums[index] = term if part == 0 else sums[index] + term
        gate_out[quarter] = sums[0]
        up_out[quarter] = sums[1]


def narrow_kernel(rows_ref, gate_ref, up_ref, *refs):
    plus, minus = refs[:2]
    down_parts = refs[2:7]
    out_ref, gate_buf, up_buf, down_buf, sems = refs[7:]
    depth = rows_ref.shape[2]
    half = down_buf.shape[2] // 2
    moves = []

    def fetch(source, target):
        move = pltpu.make_async_copy(source, target, sems.at[len(moves)])
        move.start()
        moves.append(move)

    def rows_of(ref, index):
        return ref.at[pl.ds(index * depth, depth)]

    pairs = [
        (rows_of(plus, 0), rows_of(plus, 1)),
        (rows_of(minus, 1), rows_of(minus, 2)),
        (rows_of(plus, 2), rows_of(minus, 0)),
    ]
    for index, (gate, up) in enumerate(pairs):
        fetch(gate, gate_buf.at[index])
        fetch(up, up_buf.at[index])
    for quarter in range(3):
        fetch(down_parts[quarter], down_buf.at[quarter])
    fetch(down_parts[3], down_buf.at[3, :, pl.ds(0, half)])
    fetch(down_parts[4], down_buf.at[3, :, pl.ds(half, half)])
    acts = []
    for quarter in range(4):
        gate_act, up_act = gate_ref[quarter], up_ref[quarter]
        if quarter:
            moves[2 * quarter - 2].wait()
            moves[2 * quarter - 1].wait()
            rows = rows_ref[0]
            gate_act += jnp.dot(rows, gate_buf[quarter - 1], preferred_element_type=jnp.float32)
            up_act += jnp.dot(rows, up_buf[quarter - 1], preferred_element_type=jnp.float32)
        acts.append((gate_act / (1.0 + jnp.exp(-gate_act)) * up_act).astype(jnp.bfloat16))
    for move in moves[6:]:
        move.wait()
    for part in range(PARTS):
        total = None
        for quarter in range(4):
            term = jnp.dot(
                acts[quarter],
                down_buf[quarter, :, part * depth : (part + 1) * depth],
                preferred_element_type=jnp.float32,
            )
            total = term if quarter == 0 else total + term
        out_ref[part] = total.astype(jnp.bfloat16)


def run_expert(order, rows, near_pieces, far_pieces, down_pieces):
    parts, slot_count, depth = rows.shape
    hidden_width = near_pieces[0].shape[1]
    anywhere = pl.BlockSpec(memory_space=pl.ANY)
    held = pl.BlockSpec(memory_space=pltpu.VMEM)
    act_type = jax.ShapeDtypeStruct((4, slot_count, hidden_width), jnp.float32)
    gate_part, up_part = pl.pallas_call(
        widen_kernel,
        in_specs=[
            pl.BlockSpec(memory_space=pltpu.SMEM),
            held,
            *[anywhere] * len(near_pieces),
        ],
        out_specs=[held, held],
        out_shape=[act_type, act_type],
        scratch_shapes=[
            pltpu.VMEM((4, parts, depth, hidden_width), jnp.bfloat16),
            pltpu.VMEM((4, parts, depth, hidden_width), jnp.bfloat16),
            pltpu.SemaphoreType.DMA((2 * (4 + 3 * (parts - 1)),)),
        ],
        compiler_params=pltpu.CompilerParams(vmem_limit_bytes=40 * 1024 * 1024),
        name="widen",
    )(order, rows, *near_pieces)
    return pl.pallas_call(
        narrow_kernel,
        grid=(1,),
        in_specs=[
            pl.BlockSpec((1, slot_count, depth), lambda index: (PARTS - 1, 0, 0)),
            held,
            held,
            *[anywhere] * (len(far_pieces) + len(down_pieces)),
        ],
        out_specs=held,
        out_shape=jax.ShapeDtypeStruct((parts, slot_count, depth), jnp.bfloat16),
        scratch_shapes=[
            pltpu.VMEM((3, depth, hidden_width), jnp.bfloat16),
            pltpu.VMEM((3, depth, hidden_width), jnp.bfloat16),
            pltpu.VMEM((4, hidden_width, parts * depth), jnp.bfloat16),
            pltpu.SemaphoreType.DMA((11,)),
        ],
        compiler_params=pltpu.CompilerParams(vmem_limit_bytes=40 * 1024 * 1024),
        name="narrow",
    )(rows, gate_part, up_part, *far_pieces, *down_pieces)


def body(
    queries,
    key_heads,
    value_heads,
    residual,
    out_weight,
    norm_gain,
    gate_weight,
    up_weight,
    down_weight,
    expert_ids,
    route_gates,
):
    tokens, model_width = residual.shape
    seq_size = lax.axis_size("seq")
    exp_size = lax.axis_size("exp")
    depth = model_width // PARTS
    fanout = expert_ids.shape[1]
    capacity = min(tokens, 3 * tokens * fanout // (2 * exp_size))
    slot_count = exp_size * capacity
    sent_count = PARTS * slot_count

    cand = lax.axis_index("cand")
    order = jnp.stack([cand, (cand + 3) % PARTS, (cand + 1) % PARTS, (cand + 2) % PARTS])
    seq = lax.axis_index("seq")
    head_order = jnp.stack([seq, (seq + 3) % seq_size, (seq + 1) % seq_size, (seq + 2) % seq_size])
    weight_piece = lax.dynamic_slice_in_dim(out_weight, cand * depth, depth, axis=1)
    weight_near = [shift(weight_piece, "seq", distance) for distance in (1, -1, 2)]
    own_piece = jnp.concatenate(
        [
            lax.dynamic_slice_in_dim(weight[0], cand * depth, depth, axis=0)
            for weight in (gate_weight, up_weight)
        ],
        axis=0,
    )
    before, after = shift(own_piece, "seq", 1), shift(own_piece, "seq", -1)

    pairs = jnp.concatenate(
        [
            key_heads.reshape(tokens, seq_size, HEAD_DIM),
            value_heads.reshape(tokens, seq_size, HEAD_DIM),
        ],
        axis=2,
    ).reshape(tokens, seq_size * 2 * HEAD_DIM)
    pair_local = lax.all_to_all(pairs, "seq", split_axis=1, concat_axis=0, tiled=True)
    pair_local = pair_local.reshape(seq_size, tokens, 2 * HEAD_DIM)
    query_rows = lax.all_to_all(queries, ("seq", "exp"), split_axis=1, concat_axis=0, tiled=True)
    pair_rows = lax.all_gather(pair_local, "exp", axis=1, tiled=True).reshape(
        seq_size * exp_size * tokens, 2 * HEAD_DIM
    )
    rows = weight_piece.shape[0]
    query_rows, before, after, *weight_near, weight_joined = meet(
        query_rows,
        before,
        after,
        *weight_near,
        cuts=(tuple((3 + index, 0, rows) for index in range(3)),),
    )
    other_weights = lax.all_gather(weight_joined, "cand", axis=0, tiled=True)
    attended = attend(query_rows, pair_rows)
    attended, before, after, gate_before, up_after = meet(
        attended, before, after, cuts=(((1, 0, depth),), ((2, depth, depth),))
    )
    gate_far = shift(gate_before, "seq", 1)
    up_far = shift(up_after, "seq", -1)
    head_rows = lax.all_to_all(
        attended.reshape(seq_size, -1, HEAD_DIM), "seq", split_axis=0, concat_axis=0, tiled=True
    )
    product = project(head_order, head_rows, out_weight, other_weights)
    product, gate_far, up_far = meet(product, gate_far, up_far)
    before, after, gate_far, up_far, joined = meet(
        before,
        after,
        gate_far,
        up_far,
        cuts=(((0, 0, 2 * depth), (2, 0, depth), (3, 0, depth), (1, 0, 2 * depth)),),
    )
    left, right = shift(joined, "cand", 1), shift(joined, "cand", -1)
    down_own = down_weight[0]
    down_before = shift(down_own, "seq", 1)
    down_after = shift(down_own, "seq", -1)
    half_width = model_width // 2
    low_half, high_half = down_before[:, :half_width], down_after[:, half_width:]
    projected = lax.psum_scatter(product, "exp", scatter_dimension=0, tiled=True)
    projected, left, right, low_half, high_half, plus, minus = meet(
        projected,
        left,
        right,
        low_half,
        high_half,
        cuts=(((1, 0, 3 * depth),), ((2, 3 * depth, 3 * depth),)),
    )
    plus, minus = shift(plus, "cand", 1), shift(minus, "cand", -1)
    down_far = [shift(low_half, "seq", 1), shift(high_half, "seq", -1)]
    hidden = residual.astype(jnp.float32) + projected.astype(jnp.float32)
    mean_square = jnp.mean(hidden * hidden, axis=1, keepdims=True)
    normed = (hidden * lax.rsqrt(mean_square + norm_eps) * norm_gain.astype(jnp.float32)).astype(
        jnp.bfloat16
    )

    targets = slot_targets(expert_ids, capacity)
    token_pairs = jnp.tile(targets, (PARTS, 1))
    gate_pairs = jnp.tile(route_gates, (PARTS, 1))
    pair_part = lax.broadcasted_iota(jnp.int32, (sent_count, PARTS * tokens), 1) // tokens
    slot_of, part_of = sent_rows((sent_count, PARTS * tokens), 0, capacity)
    named = [token_pairs[:, k][None, :] == slot_of for k in range(fanout)]
    turn = jnp.where(part_of == 1, 3, jnp.where(part_of == 2, 1, jnp.where(part_of == 3, 2, 0)))
    turned = (cand + turn) % PARTS
    send_map = sum((name & (turned == pair_part)).astype(jnp.float32) for name in named).astype(
        jnp.bfloat16
    )
    blend_map = sum(
        jnp.where(name & (part_of == pair_part), gate_pairs[:, k][None, :], 0.0)
        for k, name in enumerate(named)
    )
    blend_high = blend_map.astype(jnp.bfloat16)
    blend_low = (blend_map - blend_high.astype(jnp.float32)).astype(jnp.bfloat16)
    row_slot, row_part = sent_rows((sent_count, sent_count), 1, capacity)
    plain_row = lax.broadcasted_iota(jnp.int32, (sent_count, sent_count), 0)
    order_map = (plain_row == row_part * slot_count + row_slot).astype(jnp.bfloat16)

    stacked = jnp.concatenate(
        [normed[:, part * depth : (part + 1) * depth] for part in range(PARTS)], axis=0
    )
    outgoing = jnp.dot(send_map, stacked, preferred_element_type=jnp.float32).astype(jnp.bfloat16)
    arrived = lax.all_to_all(outgoing, "exp", split_axis=0, concat_axis=0, tiled=True)
    ordered = jnp.dot(order_map, arrived, preferred_element_type=jnp.float32).astype(jnp.bfloat16)
    expert_out = run_expert(
        order,
        ordered.reshape(PARTS, slot_count, depth),
        [gate_weight[0], up_weight[0], before, after, gate_far, up_far, left, right],
        [plus, minus],
        [down_own, down_before, down_after, *down_far],
    )
    leaving = lax.dot_general(
        order_map,
        expert_out.reshape(sent_count, depth),
        (((0,), (0,)), ((), ())),
        preferred_element_type=jnp.float32,
    ).astype(jnp.bfloat16)
    returned = lax.all_to_all(leaving, "exp", split_axis=0, concat_axis=0, tiled=True)
    blended = sum(
        lax.dot_general(part, returned, (((0,), (0,)), ((), ())), preferred_element_type=jnp.float32)
        for part in (blend_high, blend_low)
    )
    blended = jnp.concatenate(
        [blended[part * tokens : (part + 1) * tokens] for part in range(PARTS)], axis=1
    )
    return (hidden + blended).astype(jnp.bfloat16)


def solution(mesh):
    placed = (
        P(("cand", "seq", "exp"), None),
        P(("cand", "seq", "exp"), None),
        P(("cand", "seq", "exp"), None),
        P(("cand", "seq", "exp"), None),
        P(("seq", "exp"), None),
        P(),
        P("exp", None, "seq"),
        P("exp", None, "seq"),
        P("exp", "seq", None),
        P(("cand", "seq", "exp"), None),
        P(("cand", "seq", "exp"), None),
    )
    return jax.shard_map(
        body, mesh=mesh, in_specs=placed, out_specs=P(("cand", "seq", "exp"), None), check_vma=False
    )
```

```python
import functools
import math

import jax
import jax.numpy as jnp
from jax import lax
from jax.experimental import pallas as pl
from jax.experimental.pallas import tpu as pltpu
from jax.sharding import PartitionSpec as P

HEAD_DIM = 128
BLOCK = 512
PARTS = 4

norm_eps = 1e-06


def attention_kernel(query_ref, pair_ref, out_ref):
    factor = math.log2(math.e) / HEAD_DIM**0.5
    for start in range(0, query_ref.shape[0], BLOCK):
        seen = start + BLOCK
        scores = lax.dot_general(
            pair_ref[:seen, :HEAD_DIM],
            query_ref[start:seen, :],
            (((1,), (1,)), ((), ())),
            preferred_element_type=jnp.float32,
        )
        key_pos = lax.broadcasted_iota(jnp.int32, scores.shape, 0)
        query_pos = start + lax.broadcasted_iota(jnp.int32, scores.shape, 1)
        scores = jnp.where(key_pos <= query_pos, scores, -1e30)
        top = jnp.max(scores, axis=0, keepdims=True)
        weights = jnp.exp2(scores * factor - top * factor)
        total = jnp.sum(weights, axis=0, keepdims=True)
        mixed = lax.dot_general(
            pair_ref[:seen, HEAD_DIM:],
            weights.astype(jnp.bfloat16),
            (((0,), (0,)), ((), ())),
            preferred_element_type=jnp.float32,
        )
        out_ref[start:seen, :] = (mixed * (1.0 / total)).T.astype(jnp.bfloat16)


def attend(query_rows, pair_rows):
    whole = pl.BlockSpec(memory_space=pltpu.VMEM)
    return pl.pallas_call(
        attention_kernel,
        in_specs=[whole, whole],
        out_specs=whole,
        out_shape=jax.ShapeDtypeStruct(query_rows.shape, jnp.bfloat16),
        compiler_params=pltpu.CompilerParams(vmem_limit_bytes=48 * 1024 * 1024),
        name="attention",
    )(query_rows, pair_rows)


def slot_targets(expert_ids, capacity):
    tokens, fanout = expert_ids.shape
    entries = tokens * fanout
    flat_ids = expert_ids.reshape(entries)
    same_expert = flat_ids[:, None] == flat_ids[None, :]
    earlier = lax.broadcasted_iota(jnp.int32, (entries, entries), 1) < lax.broadcasted_iota(
        jnp.int32, (entries, entries), 0
    )
    slot_rank = jnp.sum((same_expert & earlier).astype(jnp.int32), axis=1)
    return (flat_ids * capacity + slot_rank).reshape(tokens, fanout)


def sent_rows(shape, dim, capacity):
    row = lax.broadcasted_iota(jnp.int32, shape, dim)
    within = row % (PARTS * capacity)
    return row // (PARTS * capacity) * capacity + within % capacity, within // capacity


def shift(array, axis, distance):
    size = lax.axis_size(axis)
    return lax.ppermute(array, axis, [(i, (i + distance) % size) for i in range(size)])


def meet_kernel(count, cuts, *refs):
    held = refs[:count]
    targets = refs[2 * count : 2 * count + len(cuts)]
    buffers, sems = refs[2 * count + len(cuts) : -1], refs[-1]
    used = 0
    arriving, leaving = [], []
    for buffer, cut in zip(buffers, cuts):
        row = 0
        moves = []
        for source, start, rows in cut:
            move = pltpu.make_async_copy(
                held[source].at[pl.ds(start, rows)], buffer.at[pl.ds(row, rows)], sems.at[used]
            )
            move.start()
            moves.append(move)
            row += rows
            used += 1
        arriving.append(moves)
    for target, buffer, moves in zip(targets, buffers, arriving):
        for move in moves:
            move.wait()
        move = pltpu.make_async_copy(buffer, target, sems.at[used])
        move.start()
        leaving.append(move)
        used += 1
    for move in leaving:
        move.wait()


def meet(*arrays, cuts=()):
    outside = pl.BlockSpec(memory_space=pltpu.HBM)
    held = [pltpu.HBM(array.shape, array.dtype) for array in arrays]
    shapes = [
        (sum(rows for _, _, rows in cut), arrays[cut[0][0]].shape[1]) for cut in cuts
    ]
    kinds = [arrays[cut[0][0]].dtype for cut in cuts]
    copies = sum(len(cut) + 1 for cut in cuts)
    return pl.pallas_call(
        functools.partial(meet_kernel, len(arrays), cuts),
        in_specs=[outside] * len(arrays),
        out_specs=[outside] * (len(arrays) + len(cuts)),
        out_shape=held + [pltpu.HBM(shape, kind) for shape, kind in zip(shapes, kinds)],
        input_output_aliases={index: index for index in range(len(arrays))},
        scratch_shapes=[
            *[pltpu.VMEM(shape, kind) for shape, kind in zip(shapes, kinds)],
            pltpu.SemaphoreType.DMA((max(1, copies),)),
        ],
        compiler_params=pltpu.CompilerParams(vmem_limit_bytes=16 * 1024 * 1024),
        name="meet",
    )(*arrays)


def project_kernel(order_ref, heads_ref, own_ref, others_ref, out_ref, buf, sems):
    step, last = pl.program_id(0), pl.num_programs(0) - 1
    width = buf.shape[2]
    slot = step % 2

    def leave(index, slot):
        start = pl.multiple_of(index * width, width)
        return pltpu.make_async_copy(buf.at[slot], out_ref.at[:, pl.ds(start, width)], sems.at[slot])

    @pl.when(step >= 2)
    def _():
        leave(step - 2, slot).wait()

    heads = jnp.concatenate([heads_ref[order_ref[index]] for index in range(4)], axis=1)
    weight = jnp.concatenate([own_ref[...], others_ref[...]], axis=0)
    buf[slot] = jnp.dot(heads, weight, preferred_element_type=jnp.float32).astype(jnp.bfloat16)
    leave(step, slot).start()

    @pl.when(step == last)
    def _():
        leave(step - 1, 1 - slot).wait()
        leave(step, slot).wait()


def project(order, head_rows, own_weight, other_weights):
    sources, tokens, head_dim = head_rows.shape
    width = other_weights.shape[1]
    blocks = own_weight.shape[1] // width
    others = (sources - 1) * head_dim
    return pl.pallas_call(
        project_kernel,
        grid=(blocks,),
        in_specs=[
            pl.BlockSpec(memory_space=pltpu.SMEM),
            pl.BlockSpec((sources, tokens, head_dim), lambda index: (0, 0, 0)),
            pl.BlockSpec((head_dim, width), lambda index: (0, index)),
            pl.BlockSpec((others, width), lambda index: (index, 0)),
        ],
        out_specs=pl.BlockSpec(memory_space=pltpu.HBM),
        out_shape=pltpu.HBM((tokens, blocks * width), jnp.bfloat16),
        scratch_shapes=[
            pltpu.VMEM((2, tokens, width), jnp.bfloat16),
            pltpu.SemaphoreType.DMA((2,)),
        ],
        compiler_params=pltpu.CompilerParams(vmem_limit_bytes=32 * 1024 * 1024),
        name="project",
    )(order, head_rows, own_weight, other_weights)


def widen_kernel(order_ref, rows_ref, *refs):
    gate_own, up_own, before, after, gate_far, up_far = refs[:6]
    before_sets, sets = refs[6:8], refs[8:10]
    gate_out, up_out, gate_buf, up_buf, sems = refs[10:]
    depth = rows_ref.shape[2]

    def rows_of(ref, index):
        return ref.at[pl.ds(index * depth, depth)]

    starts = [pl.multiple_of(order_ref[part] * depth, depth) for part in range(PARTS)]
    pairs = [
        [(gate_own.at[pl.ds(start, depth)], up_own.at[pl.ds(start, depth)]) for start in starts],
        [(rows_of(ref, 0), rows_of(ref, 1)) for ref in (before, *before_sets)],
        [(rows_of(after, 0), rows_of(after, 1))]
        + [(rows_of(ref, 2), rows_of(ref, 3)) for ref in sets],
        [(gate_far, up_far)] + [(rows_of(ref, 0), rows_of(ref, 1)) for ref in sets],
    ]
    moves = []
    for quarter, parts in enumerate(pairs):
        for part, sources in enumerate(parts):
            for source, target in zip(sources, (gate_buf, up_buf)):
                move = pltpu.make_async_copy(source, target.at[quarter, part], sems.at[len(moves)])
                move.start()
                moves.append(move)
    waiting = iter(moves)
    for quarter, parts in enumerate(pairs):
        sums = [None, None]
        for part in range(len(parts)):
            for index, buf in enumerate((gate_buf, up_buf)):
                next(waiting).wait()
                term = jnp.dot(
                    rows_ref[part], buf[quarter, part], preferred_element_type=jnp.float32
                )
                sums[index] = term if part == 0 else sums[index] + term
        gate_out[quarter] = sums[0]
        up_out[quarter] = sums[1]


def narrow_kernel(rows_ref, gate_ref, up_ref, *refs):
    plus, minus = refs[:2]
    down_parts = refs[2:7]
    out_ref, gate_buf, up_buf, down_buf, sems = refs[7:]
    depth = rows_ref.shape[2]
    half = down_buf.shape[2] // 2
    moves = []

    def fetch(source, target):
        move = pltpu.make_async_copy(source, target, sems.at[len(moves)])
        move.start()
        moves.append(move)

    def rows_of(ref, index):
        return ref.at[pl.ds(index * depth, depth)]

    pairs = [
        (rows_of(plus, 0), rows_of(plus, 1)),
        (rows_of(minus, 1), rows_of(minus, 2)),
        (rows_of(plus, 2), rows_of(minus, 0)),
    ]
    for index, (gate, up) in enumerate(pairs):
        fetch(gate, gate_buf.at[index])
        fetch(up, up_buf.at[index])
    for quarter in range(3):
        fetch(down_parts[quarter], down_buf.at[quarter])
    fetch(down_parts[3], down_buf.at[3, :, pl.ds(0, half)])
    fetch(down_parts[4], down_buf.at[3, :, pl.ds(half, half)])
    acts = []
    for quarter in range(4):
        gate_act, up_act = gate_ref[quarter], up_ref[quarter]
        if quarter:
            moves[2 * quarter - 2].wait()
            moves[2 * quarter - 1].wait()
            rows = rows_ref[0]
            gate_act += jnp.dot(rows, gate_buf[quarter - 1], preferred_element_type=jnp.float32)
            up_act += jnp.dot(rows, up_buf[quarter - 1], preferred_element_type=jnp.float32)
        acts.append((gate_act / (1.0 + jnp.exp(-gate_act)) * up_act).astype(jnp.bfloat16))
    for move in moves[6:]:
        move.wait()
    for part in range(PARTS):
        total = None
        for quarter in range(4):
            term = jnp.dot(
                acts[quarter],
                down_buf[quarter, :, part * depth : (part + 1) * depth],
                preferred_element_type=jnp.float32,
            )
            total = term if quarter == 0 else total + term
        out_ref[part] = total.astype(jnp.bfloat16)


def run_expert(order, rows, near_pieces, far_pieces, down_pieces):
    parts, slot_count, depth = rows.shape
    hidden_width = near_pieces[0].shape[1]
    anywhere = pl.BlockSpec(memory_space=pl.ANY)
    held = pl.BlockSpec(memory_space=pltpu.VMEM)
    act_type = jax.ShapeDtypeStruct((4, slot_count, hidden_width), jnp.float32)
    gate_part, up_part = pl.pallas_call(
        widen_kernel,
        in_specs=[
            pl.BlockSpec(memory_space=pltpu.SMEM),
            held,
            *[anywhere] * len(near_pieces),
        ],
        out_specs=[held, held],
        out_shape=[act_type, act_type],
        scratch_shapes=[
            pltpu.VMEM((4, parts, depth, hidden_width), jnp.bfloat16),
            pltpu.VMEM((4, parts, depth, hidden_width), jnp.bfloat16),
            pltpu.SemaphoreType.DMA((2 * (4 + 3 * (parts - 1)),)),
        ],
        compiler_params=pltpu.CompilerParams(vmem_limit_bytes=40 * 1024 * 1024),
        name="widen",
    )(order, rows, *near_pieces)
    return pl.pallas_call(
        narrow_kernel,
        grid=(1,),
        in_specs=[
            pl.BlockSpec((1, slot_count, depth), lambda index: (PARTS - 1, 0, 0)),
            held,
            held,
            *[anywhere] * (len(far_pieces) + len(down_pieces)),
        ],
        out_specs=held,
        out_shape=jax.ShapeDtypeStruct((parts, slot_count, depth), jnp.bfloat16),
        scratch_shapes=[
            pltpu.VMEM((3, depth, hidden_width), jnp.bfloat16),
            pltpu.VMEM((3, depth, hidden_width), jnp.bfloat16),
            pltpu.VMEM((4, hidden_width, parts * depth), jnp.bfloat16),
            pltpu.SemaphoreType.DMA((11,)),
        ],
        compiler_params=pltpu.CompilerParams(vmem_limit_bytes=40 * 1024 * 1024),
        name="narrow",
    )(rows, gate_part, up_part, *far_pieces, *down_pieces)


def body(
    queries,
    key_heads,
    value_heads,
    residual,
    out_weight,
    norm_gain,
    gate_weight,
    up_weight,
    down_weight,
    expert_ids,
    route_gates,
):
    tokens, model_width = residual.shape
    seq_size = lax.axis_size("seq")
    exp_size = lax.axis_size("exp")
    depth = model_width // PARTS
    fanout = expert_ids.shape[1]
    capacity = min(tokens, 3 * tokens * fanout // (2 * exp_size))
    slot_count = exp_size * capacity
    sent_count = PARTS * slot_count

    cand = lax.axis_index("cand")
    order = jnp.stack([cand, (cand + 3) % PARTS, (cand + 1) % PARTS, (cand + 2) % PARTS])
    seq = lax.axis_index("seq")
    head_order = jnp.stack([seq, (seq + 3) % seq_size, (seq + 1) % seq_size, (seq + 2) % seq_size])
    weight_piece = lax.dynamic_slice_in_dim(out_weight, cand * depth, depth, axis=1)
    weight_near = [shift(weight_piece, "seq", distance) for distance in (1, -1, 2)]
    own_piece = jnp.concatenate(
        [
            lax.dynamic_slice_in_dim(weight[0], cand * depth, depth, axis=0)
            for weight in (gate_weight, up_weight)
        ],
        axis=0,
    )
    before, after = shift(own_piece, "seq", 1), shift(own_piece, "seq", -1)

    pairs = jnp.concatenate(
        [
            key_heads.reshape(tokens, seq_size, HEAD_DIM),
            value_heads.reshape(tokens, seq_size, HEAD_DIM),
        ],
        axis=2,
    ).reshape(tokens, seq_size * 2 * HEAD_DIM)
    pair_local = lax.all_to_all(pairs, "seq", split_axis=1, concat_axis=0, tiled=True)
    rows = weight_piece.shape[0]
    pair_local, *weight_near, weight_joined = meet(
        pair_local, *weight_near, cuts=(tuple((1 + index, 0, rows) for index in range(3)),)
    )
    pair_local = pair_local.reshape(seq_size, tokens, 2 * HEAD_DIM)
    query_rows = lax.all_to_all(queries, ("seq", "exp"), split_axis=1, concat_axis=0, tiled=True)
    pair_rows = lax.all_gather(pair_local, "exp", axis=1, tiled=True).reshape(
        seq_size * exp_size * tokens, 2 * HEAD_DIM
    )
    other_weights = lax.all_gather(weight_joined, "cand", axis=0, tiled=True)
    attended = attend(query_rows, pair_rows)
    attended, before, after, gate_before, up_after = meet(
        attended, before, after, cuts=(((1, 0, depth),), ((2, depth, depth),))
    )
    gate_far = shift(gate_before, "seq", 1)
    up_far = shift(up_after, "seq", -1)
    before_left, before_right = shift(before, "cand", 1), shift(before, "cand", -1)
    head_rows = lax.all_to_all(
        attended.reshape(seq_size, -1, HEAD_DIM), "seq", split_axis=0, concat_axis=0, tiled=True
    )
    product = project(head_order, head_rows, out_weight, other_weights)
    product, gate_far, up_far, before_left, before_right = meet(
        product, gate_far, up_far, before_left, before_right
    )
    gate_far, up_far, after, joined = meet(
        gate_far, up_far, after, cuts=(((0, 0, depth), (1, 0, depth), (2, 0, 2 * depth)),)
    )
    left, right = shift(joined, "cand", 1), shift(joined, "cand", -1)
    down_own = down_weight[0]
    down_before = shift(down_own, "seq", 1)
    down_after = shift(down_own, "seq", -1)
    half_width = model_width // 2
    low_half, high_half = down_before[:, :half_width], down_after[:, half_width:]
    projected = lax.psum_scatter(product, "exp", scatter_dimension=0, tiled=True)
    projected, before_left, left, right, low_half, high_half, plus, minus = meet(
        projected,
        before_left,
        left,
        right,
        low_half,
        high_half,
        cuts=(((1, 0, 2 * depth), (2, 0, depth)), ((3, depth, 3 * depth),)),
    )
    plus, minus = shift(plus, "cand", 1), shift(minus, "cand", -1)
    down_far = [shift(low_half, "seq", 1), shift(high_half, "seq", -1)]
    hidden = residual.astype(jnp.float32) + projected.astype(jnp.float32)
    mean_square = jnp.mean(hidden * hidden, axis=1, keepdims=True)
    normed = (hidden * lax.rsqrt(mean_square + norm_eps) * norm_gain.astype(jnp.float32)).astype(
        jnp.bfloat16
    )

    targets = slot_targets(expert_ids, capacity)
    token_pairs = jnp.tile(targets, (PARTS, 1))
    gate_pairs = jnp.tile(route_gates, (PARTS, 1))
    pair_part = lax.broadcasted_iota(jnp.int32, (sent_count, PARTS * tokens), 1) // tokens
    slot_of, part_of = sent_rows((sent_count, PARTS * tokens), 0, capacity)
    named = [token_pairs[:, k][None, :] == slot_of for k in range(fanout)]
    turn = jnp.where(part_of == 1, 3, jnp.where(part_of == 2, 1, jnp.where(part_of == 3, 2, 0)))
    turned = (cand + turn) % PARTS
    send_map = sum((name & (turned == pair_part)).astype(jnp.float32) for name in named).astype(
        jnp.bfloat16
    )
    blend_map = sum(
        jnp.where(name & (part_of == pair_part), gate_pairs[:, k][None, :], 0.0)
        for k, name in enumerate(named)
    )
    blend_high = blend_map.astype(jnp.bfloat16)
    blend_low = (blend_map - blend_high.astype(jnp.float32)).astype(jnp.bfloat16)
    row_slot, row_part = sent_rows((sent_count, sent_count), 1, capacity)
    plain_row = lax.broadcasted_iota(jnp.int32, (sent_count, sent_count), 0)
    order_map = (plain_row == row_part * slot_count + row_slot).astype(jnp.bfloat16)

    stacked = jnp.concatenate(
        [normed[:, part * depth : (part + 1) * depth] for part in range(PARTS)], axis=0
    )
    outgoing = jnp.dot(send_map, stacked, preferred_element_type=jnp.float32).astype(jnp.bfloat16)
    arrived = lax.all_to_all(outgoing, "exp", split_axis=0, concat_axis=0, tiled=True)
    ordered = jnp.dot(order_map, arrived, preferred_element_type=jnp.float32).astype(jnp.bfloat16)
    expert_out = run_expert(
        order,
        ordered.reshape(PARTS, slot_count, depth),
        [
            *(gate_weight[0], up_weight[0], before, after, gate_far, up_far),
            *(before_left, before_right, left, right),
        ],
        [plus, minus],
        [down_own, down_before, down_after, *down_far],
    )
    leaving = lax.dot_general(
        order_map,
        expert_out.reshape(sent_count, depth),
        (((0,), (0,)), ((), ())),
        preferred_element_type=jnp.float32,
    ).astype(jnp.bfloat16)
    returned = lax.all_to_all(leaving, "exp", split_axis=0, concat_axis=0, tiled=True)
    blended = sum(
        lax.dot_general(part, returned, (((0,), (0,)), ((), ())), preferred_element_type=jnp.float32)
        for part in (blend_high, blend_low)
    )
    blended = jnp.concatenate(
        [blended[part * tokens : (part + 1) * tokens] for part in range(PARTS)], axis=1
    )
    return (hidden + blended).astype(jnp.bfloat16)


def solution(mesh):
    placed = (
        P(("cand", "seq", "exp"), None),
        P(("cand", "seq", "exp"), None),
        P(("cand", "seq", "exp"), None),
        P(("cand", "seq", "exp"), None),
        P(("seq", "exp"), None),
        P(),
        P("exp", None, "seq"),
        P("exp", None, "seq"),
        P("exp", "seq", None),
        P(("cand", "seq", "exp"), None),
        P(("cand", "seq", "exp"), None),
    )
    return jax.shard_map(
        body, mesh=mesh, in_specs=placed, out_specs=P(("cand", "seq", "exp"), None), check_vma=False
    )
```

```python
import functools
import math

import jax
import jax.numpy as jnp
from jax import lax
from jax.experimental import pallas as pl
from jax.experimental.pallas import tpu as pltpu
from jax.sharding import PartitionSpec as P

HEAD_DIM = 128
BLOCK = 512
PARTS = 4

norm_eps = 1e-06


def attention_kernel(query_ref, pair_ref, out_ref):
    factor = math.log2(math.e) / HEAD_DIM**0.5
    for start in range(0, query_ref.shape[0], BLOCK):
        seen = start + BLOCK
        scores = lax.dot_general(
            pair_ref[:seen, :HEAD_DIM],
            query_ref[start:seen, :],
            (((1,), (1,)), ((), ())),
            preferred_element_type=jnp.float32,
        )
        key_pos = lax.broadcasted_iota(jnp.int32, scores.shape, 0)
        query_pos = start + lax.broadcasted_iota(jnp.int32, scores.shape, 1)
        scores = jnp.where(key_pos <= query_pos, scores, -1e30)
        top = jnp.max(scores, axis=0, keepdims=True)
        weights = jnp.exp2(scores * factor - top * factor)
        total = jnp.sum(weights, axis=0, keepdims=True)
        mixed = lax.dot_general(
            pair_ref[:seen, HEAD_DIM:],
            weights.astype(jnp.bfloat16),
            (((0,), (0,)), ((), ())),
            preferred_element_type=jnp.float32,
        )
        out_ref[start:seen, :] = (mixed * (1.0 / total)).T.astype(jnp.bfloat16)


def attend(query_rows, pair_rows):
    whole = pl.BlockSpec(memory_space=pltpu.VMEM)
    return pl.pallas_call(
        attention_kernel,
        in_specs=[whole, whole],
        out_specs=whole,
        out_shape=jax.ShapeDtypeStruct(query_rows.shape, jnp.bfloat16),
        compiler_params=pltpu.CompilerParams(vmem_limit_bytes=48 * 1024 * 1024),
        name="attention",
    )(query_rows, pair_rows)


def slot_targets(expert_ids, capacity):
    tokens, fanout = expert_ids.shape
    entries = tokens * fanout
    flat_ids = expert_ids.reshape(entries)
    same_expert = flat_ids[:, None] == flat_ids[None, :]
    earlier = lax.broadcasted_iota(jnp.int32, (entries, entries), 1) < lax.broadcasted_iota(
        jnp.int32, (entries, entries), 0
    )
    slot_rank = jnp.sum((same_expert & earlier).astype(jnp.int32), axis=1)
    return (flat_ids * capacity + slot_rank).reshape(tokens, fanout)


def sent_rows(shape, dim, capacity):
    row = lax.broadcasted_iota(jnp.int32, shape, dim)
    within = row % (PARTS * capacity)
    return row // (PARTS * capacity) * capacity + within % capacity, within // capacity


def shift(array, axis, distance):
    size = lax.axis_size(axis)
    return lax.ppermute(array, axis, [(i, (i + distance) % size) for i in range(size)])


def meet_kernel(count, cuts, *refs):
    held = refs[:count]
    targets = refs[2 * count : 2 * count + len(cuts)]
    buffers, sems = refs[2 * count + len(cuts) : -1], refs[-1]
    used = 0
    arriving, leaving = [], []
    for buffer, cut in zip(buffers, cuts):
        row = 0
        moves = []
        for source, start, rows in cut:
            move = pltpu.make_async_copy(
                held[source].at[pl.ds(start, rows)], buffer.at[pl.ds(row, rows)], sems.at[used]
            )
            move.start()
            moves.append(move)
            row += rows
            used += 1
        arriving.append(moves)
    for target, buffer, moves in zip(targets, buffers, arriving):
        for move in moves:
            move.wait()
        move = pltpu.make_async_copy(buffer, target, sems.at[used])
        move.start()
        leaving.append(move)
        used += 1
    for move in leaving:
        move.wait()


def meet(*arrays, cuts=()):
    outside = pl.BlockSpec(memory_space=pltpu.HBM)
    held = [pltpu.HBM(array.shape, array.dtype) for array in arrays]
    shapes = [
        (sum(rows for _, _, rows in cut), arrays[cut[0][0]].shape[1]) for cut in cuts
    ]
    kinds = [arrays[cut[0][0]].dtype for cut in cuts]
    copies = sum(len(cut) + 1 for cut in cuts)
    return pl.pallas_call(
        functools.partial(meet_kernel, len(arrays), cuts),
        in_specs=[outside] * len(arrays),
        out_specs=[outside] * (len(arrays) + len(cuts)),
        out_shape=held + [pltpu.HBM(shape, kind) for shape, kind in zip(shapes, kinds)],
        input_output_aliases={index: index for index in range(len(arrays))},
        scratch_shapes=[
            *[pltpu.VMEM(shape, kind) for shape, kind in zip(shapes, kinds)],
            pltpu.SemaphoreType.DMA((max(1, copies),)),
        ],
        compiler_params=pltpu.CompilerParams(vmem_limit_bytes=16 * 1024 * 1024),
        name="meet",
    )(*arrays)


def project_kernel(head_order_ref, order_ref, heads_ref, own_ref, *refs):
    others, (out_ref, buf, sems) = refs[:PARTS], refs[PARTS:]
    width = buf.shape[2]
    heads = jnp.concatenate([heads_ref[head_order_ref[index]] for index in range(4)], axis=1)
    moves = []
    for step in range(PARTS):
        slot = step % 2
        if step >= 2:
            moves[step - 2].wait()
        start = pl.multiple_of(order_ref[step] * width, width)
        weight = jnp.concatenate([own_ref[:, pl.ds(start, width)], others[step][...]], axis=0)
        buf[slot] = jnp.dot(heads, weight, preferred_element_type=jnp.float32).astype(jnp.bfloat16)
        move = pltpu.make_async_copy(
            buf.at[slot], out_ref.at[:, pl.ds(start, width)], sems.at[slot]
        )
        move.start()
        moves.append(move)
    moves[-2].wait()
    moves[-1].wait()


def project(head_order, order, head_rows, own_weight, other_weights):
    tokens = head_rows.shape[1]
    width = other_weights[0].shape[1]
    scalars = pl.BlockSpec(memory_space=pltpu.SMEM)
    held = pl.BlockSpec(memory_space=pltpu.VMEM)
    return pl.pallas_call(
        project_kernel,
        in_specs=[scalars, scalars, *[held] * (2 + len(other_weights))],
        out_specs=pl.BlockSpec(memory_space=pltpu.HBM),
        out_shape=pltpu.HBM((tokens, own_weight.shape[1]), jnp.bfloat16),
        scratch_shapes=[
            pltpu.VMEM((2, tokens, width), jnp.bfloat16),
            pltpu.SemaphoreType.DMA((2,)),
        ],
        compiler_params=pltpu.CompilerParams(vmem_limit_bytes=32 * 1024 * 1024),
        name="project",
    )(head_order, order, head_rows, own_weight, *other_weights)


def widen_kernel(order_ref, rows_ref, *refs):
    gate_own, up_own, before, after, gate_far, up_far = refs[:6]
    before_sets, sets = refs[6:8], refs[8:10]
    gate_out, up_out, gate_buf, up_buf, sems = refs[10:]
    depth = rows_ref.shape[2]

    def rows_of(ref, index):
        return ref.at[pl.ds(index * depth, depth)]

    starts = [pl.multiple_of(order_ref[part] * depth, depth) for part in range(PARTS)]
    pairs = [
        [(gate_own.at[pl.ds(start, depth)], up_own.at[pl.ds(start, depth)]) for start in starts],
        [(rows_of(ref, 0), rows_of(ref, 1)) for ref in (before, *before_sets)],
        [(rows_of(after, 0), rows_of(after, 1))]
        + [(rows_of(ref, 2), rows_of(ref, 3)) for ref in sets],
        [(gate_far, up_far)] + [(rows_of(ref, 0), rows_of(ref, 1)) for ref in sets],
    ]
    moves = []
    for quarter, parts in enumerate(pairs):
        for part, sources in enumerate(parts):
            for source, target in zip(sources, (gate_buf, up_buf)):
                move = pltpu.make_async_copy(source, target.at[quarter, part], sems.at[len(moves)])
                move.start()
                moves.append(move)
    waiting = iter(moves)
    for quarter, parts in enumerate(pairs):
        sums = [None, None]
        for part in range(len(parts)):
            for index, buf in enumerate((gate_buf, up_buf)):
                next(waiting).wait()
                term = jnp.dot(
                    rows_ref[part], buf[quarter, part], preferred_element_type=jnp.float32
                )
                sums[index] = term if part == 0 else sums[index] + term
        gate_out[quarter] = sums[0]
        up_out[quarter] = sums[1]


def narrow_kernel(rows_ref, gate_ref, up_ref, *refs):
    plus, minus = refs[:2]
    down_parts = refs[2:7]
    out_ref, gate_buf, up_buf, down_buf, sems = refs[7:]
    depth = rows_ref.shape[2]
    half = down_buf.shape[2] // 2
    moves = []

    def fetch(source, target):
        move = pltpu.make_async_copy(source, target, sems.at[len(moves)])
        move.start()
        moves.append(move)

    def rows_of(ref, index):
        return ref.at[pl.ds(index * depth, depth)]

    pairs = [
        (rows_of(plus, 0), rows_of(plus, 1)),
        (rows_of(minus, 1), rows_of(minus, 2)),
        (rows_of(plus, 2), rows_of(minus, 0)),
    ]
    for index, (gate, up) in enumerate(pairs):
        fetch(gate, gate_buf.at[index])
        fetch(up, up_buf.at[index])
    for quarter in range(3):
        fetch(down_parts[quarter], down_buf.at[quarter])
    fetch(down_parts[3], down_buf.at[3, :, pl.ds(0, half)])
    fetch(down_parts[4], down_buf.at[3, :, pl.ds(half, half)])
    acts = []
    for quarter in range(4):
        gate_act, up_act = gate_ref[quarter], up_ref[quarter]
        if quarter:
            moves[2 * quarter - 2].wait()
            moves[2 * quarter - 1].wait()
            rows = rows_ref[0]
            gate_act += jnp.dot(rows, gate_buf[quarter - 1], preferred_element_type=jnp.float32)
            up_act += jnp.dot(rows, up_buf[quarter - 1], preferred_element_type=jnp.float32)
        acts.append((gate_act / (1.0 + jnp.exp(-gate_act)) * up_act).astype(jnp.bfloat16))
    for move in moves[6:]:
        move.wait()
    for part in range(PARTS):
        total = None
        for quarter in range(4):
            term = jnp.dot(
                acts[quarter],
                down_buf[quarter, :, part * depth : (part + 1) * depth],
                preferred_element_type=jnp.float32,
            )
            total = term if quarter == 0 else total + term
        out_ref[part] = total.astype(jnp.bfloat16)


def run_expert(order, rows, near_pieces, far_pieces, down_pieces):
    parts, slot_count, depth = rows.shape
    hidden_width = near_pieces[0].shape[1]
    anywhere = pl.BlockSpec(memory_space=pl.ANY)
    held = pl.BlockSpec(memory_space=pltpu.VMEM)
    act_type = jax.ShapeDtypeStruct((4, slot_count, hidden_width), jnp.float32)
    gate_part, up_part = pl.pallas_call(
        widen_kernel,
        in_specs=[
            pl.BlockSpec(memory_space=pltpu.SMEM),
            held,
            *[anywhere] * len(near_pieces),
        ],
        out_specs=[held, held],
        out_shape=[act_type, act_type],
        scratch_shapes=[
            pltpu.VMEM((4, parts, depth, hidden_width), jnp.bfloat16),
            pltpu.VMEM((4, parts, depth, hidden_width), jnp.bfloat16),
            pltpu.SemaphoreType.DMA((2 * (4 + 3 * (parts - 1)),)),
        ],
        compiler_params=pltpu.CompilerParams(vmem_limit_bytes=40 * 1024 * 1024),
        name="widen",
    )(order, rows, *near_pieces)
    return pl.pallas_call(
        narrow_kernel,
        grid=(1,),
        in_specs=[
            pl.BlockSpec((1, slot_count, depth), lambda index: (PARTS - 1, 0, 0)),
            held,
            held,
            *[anywhere] * (len(far_pieces) + len(down_pieces)),
        ],
        out_specs=held,
        out_shape=jax.ShapeDtypeStruct((parts, slot_count, depth), jnp.bfloat16),
        scratch_shapes=[
            pltpu.VMEM((3, depth, hidden_width), jnp.bfloat16),
            pltpu.VMEM((3, depth, hidden_width), jnp.bfloat16),
            pltpu.VMEM((4, hidden_width, parts * depth), jnp.bfloat16),
            pltpu.SemaphoreType.DMA((11,)),
        ],
        compiler_params=pltpu.CompilerParams(vmem_limit_bytes=40 * 1024 * 1024),
        name="narrow",
    )(rows, gate_part, up_part, *far_pieces, *down_pieces)


def body(
    queries,
    key_heads,
    value_heads,
    residual,
    out_weight,
    norm_gain,
    gate_weight,
    up_weight,
    down_weight,
    expert_ids,
    route_gates,
):
    tokens, model_width = residual.shape
    seq_size = lax.axis_size("seq")
    exp_size = lax.axis_size("exp")
    depth = model_width // PARTS
    fanout = expert_ids.shape[1]
    capacity = min(tokens, 3 * tokens * fanout // (2 * exp_size))
    slot_count = exp_size * capacity
    sent_count = PARTS * slot_count

    cand = lax.axis_index("cand")
    order = jnp.stack([cand, (cand + 3) % PARTS, (cand + 1) % PARTS, (cand + 2) % PARTS])
    seq = lax.axis_index("seq")
    head_order = jnp.stack([seq, (seq + 3) % seq_size, (seq + 1) % seq_size, (seq + 2) % seq_size])
    weight_piece = lax.dynamic_slice_in_dim(out_weight, cand * depth, depth, axis=1)
    weight_near = [shift(weight_piece, "seq", distance) for distance in (1, -1, 2)]
    own_piece = jnp.concatenate(
        [
            lax.dynamic_slice_in_dim(weight[0], cand * depth, depth, axis=0)
            for weight in (gate_weight, up_weight)
        ],
        axis=0,
    )
    before, after = shift(own_piece, "seq", 1), shift(own_piece, "seq", -1)

    pairs = jnp.concatenate(
        [
            key_heads.reshape(tokens, seq_size, HEAD_DIM),
            value_heads.reshape(tokens, seq_size, HEAD_DIM),
        ],
        axis=2,
    ).reshape(tokens, seq_size * 2 * HEAD_DIM)
    pair_local = lax.all_to_all(pairs, "seq", split_axis=1, concat_axis=0, tiled=True)
    rows = weight_piece.shape[0]
    pair_local, *weight_near, weight_joined = meet(
        pair_local, *weight_near, cuts=(tuple((1 + index, 0, rows) for index in range(3)),)
    )
    weight_others = [shift(weight_joined, "cand", distance) for distance in (1, -1, 2)]
    pair_local = pair_local.reshape(seq_size, tokens, 2 * HEAD_DIM)
    query_rows = lax.all_to_all(queries, ("seq", "exp"), split_axis=1, concat_axis=0, tiled=True)
    pair_rows = lax.all_gather(pair_local, "exp", axis=1, tiled=True).reshape(
        seq_size * exp_size * tokens, 2 * HEAD_DIM
    )
    attended = attend(query_rows, pair_rows)
    attended, before, after, *weight_others, gate_before, up_after = meet(
        attended,
        before,
        after,
        *weight_others,
        cuts=(((1, 0, depth),), ((2, depth, depth),)),
    )
    gate_far = shift(gate_before, "seq", 1)
    up_far = shift(up_after, "seq", -1)
    before_left, before_right = shift(before, "cand", 1), shift(before, "cand", -1)
    head_rows = lax.all_to_all(
        attended.reshape(seq_size, -1, HEAD_DIM), "seq", split_axis=0, concat_axis=0, tiled=True
    )
    product = project(head_order, order, head_rows, out_weight, [weight_joined, *weight_others])
    product, gate_far, up_far, before_left, before_right = meet(
        product, gate_far, up_far, before_left, before_right
    )
    gate_far, up_far, after, joined = meet(
        gate_far, up_far, after, cuts=(((0, 0, depth), (1, 0, depth), (2, 0, 2 * depth)),)
    )
    left, right = shift(joined, "cand", 1), shift(joined, "cand", -1)
    down_own = down_weight[0]
    down_before = shift(down_own, "seq", 1)
    down_after = shift(down_own, "seq", -1)
    half_width = model_width // 2
    low_half, high_half = down_before[:, :half_width], down_after[:, half_width:]
    projected = lax.psum_scatter(product, "exp", scatter_dimension=0, tiled=True)
    projected, before_left, left, right, low_half, high_half, plus, minus = meet(
        projected,
        before_left,
        left,
        right,
        low_half,
        high_half,
        cuts=(((1, 0, 2 * depth), (2, 0, depth)), ((3, depth, 3 * depth),)),
    )
    plus, minus = shift(plus, "cand", 1), shift(minus, "cand", -1)
    down_far = [shift(low_half, "seq", 1), shift(high_half, "seq", -1)]
    hidden = residual.astype(jnp.float32) + projected.astype(jnp.float32)
    mean_square = jnp.mean(hidden * hidden, axis=1, keepdims=True)
    normed = (hidden * lax.rsqrt(mean_square + norm_eps) * norm_gain.astype(jnp.float32)).astype(
        jnp.bfloat16
    )

    targets = slot_targets(expert_ids, capacity)
    token_pairs = jnp.tile(targets, (PARTS, 1))
    gate_pairs = jnp.tile(route_gates, (PARTS, 1))
    pair_part = lax.broadcasted_iota(jnp.int32, (sent_count, PARTS * tokens), 1) // tokens
    slot_of, part_of = sent_rows((sent_count, PARTS * tokens), 0, capacity)
    named = [token_pairs[:, k][None, :] == slot_of for k in range(fanout)]
    turn = jnp.where(part_of == 1, 3, jnp.where(part_of == 2, 1, jnp.where(part_of == 3, 2, 0)))
    turned = (cand + turn) % PARTS
    send_map = sum((name & (turned == pair_part)).astype(jnp.float32) for name in named).astype(
        jnp.bfloat16
    )
    blend_map = sum(
        jnp.where(name & (part_of == pair_part), gate_pairs[:, k][None, :], 0.0)
        for k, name in enumerate(named)
    )
    blend_high = blend_map.astype(jnp.bfloat16)
    blend_low = (blend_map - blend_high.astype(jnp.float32)).astype(jnp.bfloat16)
    row_slot, row_part = sent_rows((sent_count, sent_count), 1, capacity)
    plain_row = lax.broadcasted_iota(jnp.int32, (sent_count, sent_count), 0)
    order_map = (plain_row == row_part * slot_count + row_slot).astype(jnp.bfloat16)

    stacked = jnp.concatenate(
        [normed[:, part * depth : (part + 1) * depth] for part in range(PARTS)], axis=0
    )
    outgoing = jnp.dot(send_map, stacked, preferred_element_type=jnp.float32).astype(jnp.bfloat16)
    arrived = lax.all_to_all(outgoing, "exp", split_axis=0, concat_axis=0, tiled=True)
    ordered = jnp.dot(order_map, arrived, preferred_element_type=jnp.float32).astype(jnp.bfloat16)
    expert_out = run_expert(
        order,
        ordered.reshape(PARTS, slot_count, depth),
        [
            *(gate_weight[0], up_weight[0], before, after, gate_far, up_far),
            *(before_left, before_right, left, right),
        ],
        [plus, minus],
        [down_own, down_before, down_after, *down_far],
    )
    leaving = lax.dot_general(
        order_map,
        expert_out.reshape(sent_count, depth),
        (((0,), (0,)), ((), ())),
        preferred_element_type=jnp.float32,
    ).astype(jnp.bfloat16)
    returned = lax.all_to_all(leaving, "exp", split_axis=0, concat_axis=0, tiled=True)
    blended = sum(
        lax.dot_general(part, returned, (((0,), (0,)), ((), ())), preferred_element_type=jnp.float32)
        for part in (blend_high, blend_low)
    )
    blended = jnp.concatenate(
        [blended[part * tokens : (part + 1) * tokens] for part in range(PARTS)], axis=1
    )
    return (hidden + blended).astype(jnp.bfloat16)


def solution(mesh):
    placed = (
        P(("cand", "seq", "exp"), None),
        P(("cand", "seq", "exp"), None),
        P(("cand", "seq", "exp"), None),
        P(("cand", "seq", "exp"), None),
        P(("seq", "exp"), None),
        P(),
        P("exp", None, "seq"),
        P("exp", None, "seq"),
        P("exp", "seq", None),
        P(("cand", "seq", "exp"), None),
        P(("cand", "seq", "exp"), None),
    )
    return jax.shard_map(
        body, mesh=mesh, in_specs=placed, out_specs=P(("cand", "seq", "exp"), None), check_vma=False
    )
```

```python
import functools
import math

import jax
import jax.numpy as jnp
from jax import lax
from jax.experimental import pallas as pl
from jax.experimental.pallas import tpu as pltpu
from jax.sharding import PartitionSpec as P

HEAD_DIM = 128
BLOCK = 512
PARTS = 4

norm_eps = 1e-06


def attention_kernel(query_ref, pair_ref, out_ref):
    factor = math.log2(math.e) / HEAD_DIM**0.5
    for start in range(0, query_ref.shape[0], BLOCK):
        seen = start + BLOCK
        scores = lax.dot_general(
            pair_ref[:seen, :HEAD_DIM],
            query_ref[start:seen, :],
            (((1,), (1,)), ((), ())),
            preferred_element_type=jnp.float32,
        )
        key_pos = lax.broadcasted_iota(jnp.int32, scores.shape, 0)
        query_pos = start + lax.broadcasted_iota(jnp.int32, scores.shape, 1)
        scores = jnp.where(key_pos <= query_pos, scores, -1e30)
        top = jnp.max(scores, axis=0, keepdims=True)
        weights = jnp.exp2(scores * factor - top * factor)
        total = jnp.sum(weights, axis=0, keepdims=True)
        mixed = lax.dot_general(
            pair_ref[:seen, HEAD_DIM:],
            weights.astype(jnp.bfloat16),
            (((0,), (0,)), ((), ())),
            preferred_element_type=jnp.float32,
        )
        out_ref[start:seen, :] = (mixed * (1.0 / total)).T.astype(jnp.bfloat16)


def attend(query_rows, pair_rows):
    whole = pl.BlockSpec(memory_space=pltpu.VMEM)
    return pl.pallas_call(
        attention_kernel,
        in_specs=[whole, whole],
        out_specs=whole,
        out_shape=jax.ShapeDtypeStruct(query_rows.shape, jnp.bfloat16),
        compiler_params=pltpu.CompilerParams(vmem_limit_bytes=48 * 1024 * 1024),
        name="attention",
    )(query_rows, pair_rows)


def slot_targets(expert_ids, capacity):
    tokens, fanout = expert_ids.shape
    entries = tokens * fanout
    flat_ids = expert_ids.reshape(entries)
    same_expert = flat_ids[:, None] == flat_ids[None, :]
    earlier = lax.broadcasted_iota(jnp.int32, (entries, entries), 1) < lax.broadcasted_iota(
        jnp.int32, (entries, entries), 0
    )
    slot_rank = jnp.sum((same_expert & earlier).astype(jnp.int32), axis=1)
    return (flat_ids * capacity + slot_rank).reshape(tokens, fanout)


def sent_rows(shape, dim, capacity):
    row = lax.broadcasted_iota(jnp.int32, shape, dim)
    within = row % (PARTS * capacity)
    return row // (PARTS * capacity) * capacity + within % capacity, within // capacity


def shift(array, axis, distance):
    size = lax.axis_size(axis)
    return lax.ppermute(array, axis, [(i, (i + distance) % size) for i in range(size)])


def meet_kernel(count, cuts, *refs):
    held = refs[:count]
    targets = refs[2 * count : 2 * count + len(cuts)]
    buffers, sems = refs[2 * count + len(cuts) : -1], refs[-1]
    used = 0
    arriving, leaving = [], []
    for buffer, cut in zip(buffers, cuts):
        row = 0
        moves = []
        for source, start, rows in cut:
            move = pltpu.make_async_copy(
                held[source].at[pl.ds(start, rows)], buffer.at[pl.ds(row, rows)], sems.at[used]
            )
            move.start()
            moves.append(move)
            row += rows
            used += 1
        arriving.append(moves)
    for target, buffer, moves in zip(targets, buffers, arriving):
        for move in moves:
            move.wait()
        move = pltpu.make_async_copy(buffer, target, sems.at[used])
        move.start()
        leaving.append(move)
        used += 1
    for move in leaving:
        move.wait()


def meet(*arrays, cuts=()):
    outside = pl.BlockSpec(memory_space=pltpu.HBM)
    held = [pltpu.HBM(array.shape, array.dtype) for array in arrays]
    shapes = [
        (sum(rows for _, _, rows in cut), arrays[cut[0][0]].shape[1]) for cut in cuts
    ]
    kinds = [arrays[cut[0][0]].dtype for cut in cuts]
    copies = sum(len(cut) + 1 for cut in cuts)
    return pl.pallas_call(
        functools.partial(meet_kernel, len(arrays), cuts),
        in_specs=[outside] * len(arrays),
        out_specs=[outside] * (len(arrays) + len(cuts)),
        out_shape=held + [pltpu.HBM(shape, kind) for shape, kind in zip(shapes, kinds)],
        input_output_aliases={index: index for index in range(len(arrays))},
        scratch_shapes=[
            *[pltpu.VMEM(shape, kind) for shape, kind in zip(shapes, kinds)],
            pltpu.SemaphoreType.DMA((max(1, copies),)),
        ],
        compiler_params=pltpu.CompilerParams(vmem_limit_bytes=16 * 1024 * 1024),
        name="meet",
    )(*arrays)


def project_kernel(head_order_ref, order_ref, heads_ref, own_ref, *refs):
    others, (out_ref, buf, sems) = refs[:PARTS], refs[PARTS:]
    width = buf.shape[2]
    heads = jnp.concatenate([heads_ref[head_order_ref[index]] for index in range(4)], axis=1)
    moves = []
    for step in range(PARTS):
        slot = step % 2
        if step >= 2:
            moves[step - 2].wait()
        start = pl.multiple_of(order_ref[step] * width, width)
        weight = jnp.concatenate([own_ref[:, pl.ds(start, width)], others[step][...]], axis=0)
        buf[slot] = jnp.dot(heads, weight, preferred_element_type=jnp.float32).astype(jnp.bfloat16)
        move = pltpu.make_async_copy(
            buf.at[slot], out_ref.at[:, pl.ds(start, width)], sems.at[slot]
        )
        move.start()
        moves.append(move)
    moves[-2].wait()
    moves[-1].wait()


def project(head_order, order, head_rows, own_weight, other_weights):
    tokens = head_rows.shape[1]
    width = other_weights[0].shape[1]
    scalars = pl.BlockSpec(memory_space=pltpu.SMEM)
    held = pl.BlockSpec(memory_space=pltpu.VMEM)
    return pl.pallas_call(
        project_kernel,
        in_specs=[scalars, scalars, *[held] * (2 + len(other_weights))],
        out_specs=pl.BlockSpec(memory_space=pltpu.HBM),
        out_shape=pltpu.HBM((tokens, own_weight.shape[1]), jnp.bfloat16),
        scratch_shapes=[
            pltpu.VMEM((2, tokens, width), jnp.bfloat16),
            pltpu.SemaphoreType.DMA((2,)),
        ],
        compiler_params=pltpu.CompilerParams(vmem_limit_bytes=32 * 1024 * 1024),
        name="project",
    )(head_order, order, head_rows, own_weight, *other_weights)


def widen_kernel(order_ref, rows_ref, *refs):
    gate_own, up_own, before, after, gate_far, up_far = refs[:6]
    before_sets, sets = refs[6:8], refs[8:10]
    gate_out, up_out, gate_buf, up_buf, sems = refs[10:]
    depth = rows_ref.shape[2]

    def rows_of(ref, index):
        return ref.at[pl.ds(index * depth, depth)]

    starts = [pl.multiple_of(order_ref[part] * depth, depth) for part in range(PARTS)]
    pairs = [
        [(gate_own.at[pl.ds(start, depth)], up_own.at[pl.ds(start, depth)]) for start in starts],
        [(rows_of(ref, 0), rows_of(ref, 1)) for ref in (before, *before_sets)],
        [(rows_of(after, 0), rows_of(after, 1))]
        + [(rows_of(ref, 2), rows_of(ref, 3)) for ref in sets],
        [(gate_far, up_far)] + [(rows_of(ref, 0), rows_of(ref, 1)) for ref in sets],
    ]
    moves = []
    for quarter, parts in enumerate(pairs):
        for part, sources in enumerate(parts):
            for source, target in zip(sources, (gate_buf, up_buf)):
                move = pltpu.make_async_copy(source, target.at[quarter, part], sems.at[len(moves)])
                move.start()
                moves.append(move)
    waiting = iter(moves)
    for quarter, parts in enumerate(pairs):
        sums = [None, None]
        for part in range(len(parts)):
            for index, buf in enumerate((gate_buf, up_buf)):
                next(waiting).wait()
                term = jnp.dot(
                    rows_ref[part], buf[quarter, part], preferred_element_type=jnp.float32
                )
                sums[index] = term if part == 0 else sums[index] + term
        gate_out[quarter] = sums[0]
        up_out[quarter] = sums[1]


def narrow_kernel(rows_ref, gate_ref, up_ref, *refs):
    plus, minus = refs[:2]
    down_parts = refs[2:7]
    out_ref, gate_buf, up_buf, down_buf, sems = refs[7:]
    depth = rows_ref.shape[2]
    half = down_buf.shape[1] // 2
    moves = []

    def fetch(source, target):
        move = pltpu.make_async_copy(source, target, sems.at[len(moves)])
        move.start()
        moves.append(move)

    def rows_of(ref, index):
        return ref.at[pl.ds(index * depth, depth)]

    pairs = [
        (rows_of(plus, 0), rows_of(plus, 1)),
        (rows_of(minus, 1), rows_of(minus, 2)),
        (rows_of(plus, 2), rows_of(minus, 0)),
    ]
    for index, (gate, up) in enumerate(pairs):
        fetch(gate, gate_buf.at[index])
        fetch(up, up_buf.at[index])
    for quarter in range(3):
        fetch(down_parts[quarter], down_buf.at[quarter])
    fetch(down_parts[3], down_buf.at[3, pl.ds(0, half)])
    fetch(down_parts[4], down_buf.at[3, pl.ds(half, half)])
    acts = []
    for quarter in range(4):
        gate_act, up_act = gate_ref[quarter], up_ref[quarter]
        if quarter:
            moves[2 * quarter - 2].wait()
            moves[2 * quarter - 1].wait()
            rows = rows_ref[0]
            gate_act += jnp.dot(rows, gate_buf[quarter - 1], preferred_element_type=jnp.float32)
            up_act += jnp.dot(rows, up_buf[quarter - 1], preferred_element_type=jnp.float32)
        acts.append((gate_act / (1.0 + jnp.exp(-gate_act)) * up_act).astype(jnp.bfloat16))
    for move in moves[6:]:
        move.wait()
    for part in range(PARTS):
        total = None
        for quarter in range(4):
            term = jnp.dot(
                acts[quarter],
                down_buf[quarter, :, part * depth : (part + 1) * depth],
                preferred_element_type=jnp.float32,
            )
            total = term if quarter == 0 else total + term
        out_ref[part] = total.astype(jnp.bfloat16)


def run_expert(order, rows, near_pieces, far_pieces, down_pieces):
    parts, slot_count, depth = rows.shape
    hidden_width = near_pieces[0].shape[1]
    anywhere = pl.BlockSpec(memory_space=pl.ANY)
    held = pl.BlockSpec(memory_space=pltpu.VMEM)
    act_type = jax.ShapeDtypeStruct((4, slot_count, hidden_width), jnp.float32)
    gate_part, up_part = pl.pallas_call(
        widen_kernel,
        in_specs=[
            pl.BlockSpec(memory_space=pltpu.SMEM),
            held,
            *[anywhere] * len(near_pieces),
        ],
        out_specs=[held, held],
        out_shape=[act_type, act_type],
        scratch_shapes=[
            pltpu.VMEM((4, parts, depth, hidden_width), jnp.bfloat16),
            pltpu.VMEM((4, parts, depth, hidden_width), jnp.bfloat16),
            pltpu.SemaphoreType.DMA((2 * (4 + 3 * (parts - 1)),)),
        ],
        compiler_params=pltpu.CompilerParams(vmem_limit_bytes=40 * 1024 * 1024),
        name="widen",
    )(order, rows, *near_pieces)
    return pl.pallas_call(
        narrow_kernel,
        grid=(1,),
        in_specs=[
            pl.BlockSpec((1, slot_count, depth), lambda index: (PARTS - 1, 0, 0)),
            held,
            held,
            *[anywhere] * (len(far_pieces) + len(down_pieces)),
        ],
        out_specs=held,
        out_shape=jax.ShapeDtypeStruct((parts, slot_count, depth), jnp.bfloat16),
        scratch_shapes=[
            pltpu.VMEM((3, depth, hidden_width), jnp.bfloat16),
            pltpu.VMEM((3, depth, hidden_width), jnp.bfloat16),
            pltpu.VMEM((4, hidden_width, parts * depth), jnp.bfloat16),
            pltpu.SemaphoreType.DMA((11,)),
        ],
        compiler_params=pltpu.CompilerParams(vmem_limit_bytes=40 * 1024 * 1024),
        name="narrow",
    )(rows, gate_part, up_part, *far_pieces, *down_pieces)


def body(
    queries,
    key_heads,
    value_heads,
    residual,
    out_weight,
    norm_gain,
    gate_weight,
    up_weight,
    down_weight,
    expert_ids,
    route_gates,
):
    tokens, model_width = residual.shape
    seq_size = lax.axis_size("seq")
    exp_size = lax.axis_size("exp")
    depth = model_width // PARTS
    fanout = expert_ids.shape[1]
    capacity = min(tokens, 3 * tokens * fanout // (2 * exp_size))
    slot_count = exp_size * capacity
    sent_count = PARTS * slot_count

    cand = lax.axis_index("cand")
    order = jnp.stack([cand, (cand + 3) % PARTS, (cand + 1) % PARTS, (cand + 2) % PARTS])
    seq = lax.axis_index("seq")
    head_order = jnp.stack([seq, (seq + 3) % seq_size, (seq + 1) % seq_size, (seq + 2) % seq_size])
    weight_piece = lax.dynamic_slice_in_dim(out_weight, cand * depth, depth, axis=1)
    weight_near = [shift(weight_piece, "seq", distance) for distance in (1, -1, 2)]
    own_piece = jnp.concatenate(
        [
            lax.dynamic_slice_in_dim(weight[0], cand * depth, depth, axis=0)
            for weight in (gate_weight, up_weight)
        ],
        axis=0,
    )
    before, after = shift(own_piece, "seq", 1), shift(own_piece, "seq", -1)

    pairs = jnp.concatenate(
        [
            key_heads.reshape(tokens, seq_size, HEAD_DIM),
            value_heads.reshape(tokens, seq_size, HEAD_DIM),
        ],
        axis=2,
    ).reshape(tokens, seq_size * 2 * HEAD_DIM)
    pair_local = lax.all_to_all(pairs, "seq", split_axis=1, concat_axis=0, tiled=True)
    rows = weight_piece.shape[0]
    pair_local, *weight_near, weight_joined = meet(
        pair_local, *weight_near, cuts=(tuple((1 + index, 0, rows) for index in range(3)),)
    )
    weight_others = [shift(weight_joined, "cand", distance) for distance in (1, -1, 2)]
    pair_local = pair_local.reshape(seq_size, tokens, 2 * HEAD_DIM)
    query_rows = lax.all_to_all(queries, ("seq", "exp"), split_axis=1, concat_axis=0, tiled=True)
    pair_rows = lax.all_gather(pair_local, "exp", axis=1, tiled=True).reshape(
        seq_size * exp_size * tokens, 2 * HEAD_DIM
    )
    attended = attend(query_rows, pair_rows)
    attended, before, after, *weight_others, gate_before, up_after = meet(
        attended,
        before,
        after,
        *weight_others,
        cuts=(((1, 0, depth),), ((2, depth, depth),)),
    )
    gate_far = shift(gate_before, "seq", 1)
    up_far = shift(up_after, "seq", -1)
    before_left, before_right = shift(before, "cand", 1), shift(before, "cand", -1)
    head_rows = lax.all_to_all(
        attended.reshape(seq_size, -1, HEAD_DIM), "seq", split_axis=0, concat_axis=0, tiled=True
    )
    product = project(head_order, order, head_rows, out_weight, [weight_joined, *weight_others])
    product, gate_far, up_far, before_left, before_right = meet(
        product, gate_far, up_far, before_left, before_right
    )
    gate_far, up_far, after, joined = meet(
        gate_far, up_far, after, cuts=(((0, 0, depth), (1, 0, depth), (2, 0, 2 * depth)),)
    )
    left, right = shift(joined, "cand", 1), shift(joined, "cand", -1)
    down_own = down_weight[0]
    down_before = shift(down_own, "seq", 1)
    down_after = shift(down_own, "seq", -1)
    projected = lax.psum_scatter(product, "exp", scatter_dimension=0, tiled=True)
    projected, before_left, left, right, down_before, down_after = meet(
        projected, before_left, left, right, down_before, down_after
    )
    half_rows = down_own.shape[0] // 2
    before_left, left, right, down_before, down_after, plus, minus, low_half, high_half = meet(
        before_left,
        left,
        right,
        down_before,
        down_after,
        cuts=(
            ((0, 0, 2 * depth), (1, 0, depth)),
            ((2, depth, 3 * depth),),
            ((3, 0, half_rows),),
            ((4, half_rows, half_rows),),
        ),
    )
    plus, minus = shift(plus, "cand", 1), shift(minus, "cand", -1)
    down_far = [shift(low_half, "seq", 1), shift(high_half, "seq", -1)]
    hidden = residual.astype(jnp.float32) + projected.astype(jnp.float32)
    mean_square = jnp.mean(hidden * hidden, axis=1, keepdims=True)
    normed = (hidden * lax.rsqrt(mean_square + norm_eps) * norm_gain.astype(jnp.float32)).astype(
        jnp.bfloat16
    )

    targets = slot_targets(expert_ids, capacity)
    token_pairs = jnp.tile(targets, (PARTS, 1))
    gate_pairs = jnp.tile(route_gates, (PARTS, 1))
    pair_part = lax.broadcasted_iota(jnp.int32, (sent_count, PARTS * tokens), 1) // tokens
    slot_of, part_of = sent_rows((sent_count, PARTS * tokens), 0, capacity)
    named = [token_pairs[:, k][None, :] == slot_of for k in range(fanout)]
    turn = jnp.where(part_of == 1, 3, jnp.where(part_of == 2, 1, jnp.where(part_of == 3, 2, 0)))
    turned = (cand + turn) % PARTS
    send_map = sum((name & (turned == pair_part)).astype(jnp.float32) for name in named).astype(
        jnp.bfloat16
    )
    blend_map = sum(
        jnp.where(name & (part_of == pair_part), gate_pairs[:, k][None, :], 0.0)
        for k, name in enumerate(named)
    )
    blend_high = blend_map.astype(jnp.bfloat16)
    blend_low = (blend_map - blend_high.astype(jnp.float32)).astype(jnp.bfloat16)
    row_slot, row_part = sent_rows((sent_count, sent_count), 1, capacity)
    plain_row = lax.broadcasted_iota(jnp.int32, (sent_count, sent_count), 0)
    order_map = (plain_row == row_part * slot_count + row_slot).astype(jnp.bfloat16)

    stacked = jnp.concatenate(
        [normed[:, part * depth : (part + 1) * depth] for part in range(PARTS)], axis=0
    )
    outgoing = jnp.dot(send_map, stacked, preferred_element_type=jnp.float32).astype(jnp.bfloat16)
    arrived = lax.all_to_all(outgoing, "exp", split_axis=0, concat_axis=0, tiled=True)
    ordered = jnp.dot(order_map, arrived, preferred_element_type=jnp.float32).astype(jnp.bfloat16)
    expert_out = run_expert(
        order,
        ordered.reshape(PARTS, slot_count, depth),
        [
            *(gate_weight[0], up_weight[0], before, after, gate_far, up_far),
            *(before_left, before_right, left, right),
        ],
        [plus, minus],
        [down_own, down_before, down_after, *down_far],
    )
    leaving = lax.dot_general(
        order_map,
        expert_out.reshape(sent_count, depth),
        (((0,), (0,)), ((), ())),
        preferred_element_type=jnp.float32,
    ).astype(jnp.bfloat16)
    returned = lax.all_to_all(leaving, "exp", split_axis=0, concat_axis=0, tiled=True)
    blended = sum(
        lax.dot_general(part, returned, (((0,), (0,)), ((), ())), preferred_element_type=jnp.float32)
        for part in (blend_high, blend_low)
    )
    blended = jnp.concatenate(
        [blended[part * tokens : (part + 1) * tokens] for part in range(PARTS)], axis=1
    )
    return (hidden + blended).astype(jnp.bfloat16)


def solution(mesh):
    placed = (
        P(("cand", "seq", "exp"), None),
        P(("cand", "seq", "exp"), None),
        P(("cand", "seq", "exp"), None),
        P(("cand", "seq", "exp"), None),
        P(("seq", "exp"), None),
        P(),
        P("exp", None, "seq"),
        P("exp", None, "seq"),
        P("exp", "seq", None),
        P(("cand", "seq", "exp"), None),
        P(("cand", "seq", "exp"), None),
    )
    return jax.shard_map(
        body, mesh=mesh, in_specs=placed, out_specs=P(("cand", "seq", "exp"), None), check_vma=False
    )
```
